32 devices in a mesh: px: 8 (over z, y), py: 4 (over x, core).
Axes of the slice: x: 2, y: 2, z: 4, core: 2. Of those that a mesh axis runs over, the one named last changes fastest.
Arguments:
- flow_state: float32 [5, 64, 8, 32, 128], P(None, None, 'px', 'py'), may hold values from -1 to 3.2, as said below
- adjoint: float32 [5, 64, 8, 32, 128], P(None, None, 'px', 'py'), may hold values from -6 to 6
- displacement: float32 [3, 16, 36, 128], P(None, 'px', 'py'), may hold values from -0.1 to 0.1, as said below
- lattice_block: int32 [8, 4, 1024, 1], P('px', 'py'), may hold values from 0 to 31; in each aligned block of 1024 rows (0 to 1023, 1024 to 2047, ..., all dimensions but the last counted through in order) at most 64 rows name the same one
- lattice_coords: float32 [8, 4, 3, 1024], P('px', 'py'), may hold values from 0.02 to 0.98
Outputs:
- adjoint_residual: float32 [5, 64, 8, 32, 128], P(None, None, 'px', 'py')
- owned_vertex_sensitivity: float32 [3, 8, 32, 128], P(None, 'px', 'py')
- lattice_grad: float32 [8, 4, 3, 864], P('px', 'py')
The draws below stay inside these ranges and needn't reach their ends.
Inputs may be any that keep to these rules, and one draw needn't show every extreme that they name: `flow_state`: field 0 (density) lies in 0.8 to 1.25, fields 1 to 3 (momenta) in -1 to 1, field 4 (energy) in 2 to 3.2. `displacement`: each device stores the vertex layers at both ends of its block along the first two dimensions; a vertex stored by two devices has equal values in both copies. `lattice_block`: among the 1024 vertices of one device no lattice block is named more than 64 times, and in some devices one block is named exactly 64 times.
All inputs are finite; a program needn't handle non-finite values.
Results may differ from the reference program's by a relative error of at most 0.0003.
Values sent between devices are 32-bit elements; how exact they have to be, the bound alone decides.
No kernel may reach another device: no remote copies, remote signals or barrier semaphores. Data moves between devices by JAX's collectives and lax.ppermute only.
A program may use at most 128 MiB of HBM per device.

```python
import math
import jax
import jax.numpy as jnp
import numpy as np
from jax import lax

DEVICE_ELEMS_X = 1
DEVICE_ELEMS_Y = 8
LU = 12
LV = 12
LW = 6
ELEMENTS_FIRST = 8
ELEMENTS_SECOND = 32
ELEMENTS_THIRD = 128
DEVICE_VERTICES = 1024
LATTICE_BLOCKS = 32
CAP = 64
LPTS = 864
N_PX = 8
N_PY = 4


def draw_flow_state(key, part):
    subkeys = jax.random.split(key, 3)
    reference_layout = (64, ELEMENTS_FIRST, ELEMENTS_SECOND, ELEMENTS_THIRD)
    density = jax.random.uniform(subkeys[0], reference_layout, jnp.float32, 0.85, 1.2)
    momentum = jnp.clip(0.3 * jax.random.normal(subkeys[1], (3,) + reference_layout, jnp.float32), -1.0, 1.0)
    energy = jax.random.uniform(subkeys[2], reference_layout, jnp.float32, 2.2, 3.0)
    return jnp.concatenate([density[None], momentum, energy[None]], axis=0)


def draw_displacement(key, part):
    reference_layout = (3, ELEMENTS_FIRST + 1, ELEMENTS_SECOND, ELEMENTS_THIRD)
    base_field = jnp.clip(0.04 * jax.random.normal(key, reference_layout, jnp.float32), -0.1, 0.1)
    stored_x = jnp.arange((DEVICE_ELEMS_X + 1) * (ELEMENTS_FIRST // DEVICE_ELEMS_X), dtype=jnp.int32)
    xindex = (stored_x // (DEVICE_ELEMS_X + 1) * DEVICE_ELEMS_X + stored_x % (DEVICE_ELEMS_X + 1)).astype(jnp.int32)
    stored_y = jnp.arange((DEVICE_ELEMS_Y + 1) * (ELEMENTS_SECOND // DEVICE_ELEMS_Y), dtype=jnp.int32)
    yindex = ((stored_y // (DEVICE_ELEMS_Y + 1) * DEVICE_ELEMS_Y + stored_y % (DEVICE_ELEMS_Y + 1)) % ELEMENTS_SECOND).astype(jnp.int32)
    return jnp.take(jnp.take(base_field, xindex, axis=1), yindex, axis=2)


def shard_levels(key, extent, cuts, low, largest):
    def one(axis_at, shards_of):
        draws = jax.random.uniform(jax.random.fold_in(jax.random.fold_in(key, 6), axis_at), (shards_of,), jnp.float32, low / len(cuts), largest / len(cuts))
        return jnp.repeat(jnp.exp(draws), extent[axis_at] // shards_of).reshape((-1,) + (1,) * (len(extent) - axis_at - 1))

    loudness = one(*cuts[0])
    for cut in cuts[1:]:
        loudness = loudness * one(*cut)
    return loudness


def deal_out(key, own, number, rows, amount, top, bound, lean):
    sequence = jax.random.permutation(key, amount)
    crowded, ordinary = load_shares(amount, rows * top, bound, lean, True), load_shares(amount, rows * top, bound, lean, False)
    places = jnp.arange(amount)

    def named(lengths, rotation):
        used = int((lengths > 0).sum())
        fixed = max(1, used // 4)
        shifted = fixed + (places - fixed + rotation * (used - fixed)) % max(1, amount - fixed)
        return jnp.zeros((amount,), jnp.int32).at[sequence[jnp.where(places < fixed, places, shifted)]].set(jnp.asarray(lengths, jnp.int32))

    lengths = jnp.where(number % 4 == 0, named(crowded, number // 4), named(ordinary, number - number // 4 - 1))
    mixed = jax.random.permutation(jax.random.fold_in(own, 3), amount)
    donor, taker = mixed[0:amount // 2 * 2:2], mixed[1:amount // 2 * 2:2]
    margin = jnp.minimum(lengths[donor] - 1, bound - lengths[taker]) // 2
    margin = jnp.where((donor == sequence[0]) | (taker == sequence[0]) | (lengths[taker] == 0), 0, jnp.maximum(margin, 0))
    shifted = jax.random.randint(jax.random.fold_in(own, 4), (amount // 2,), 0, 1 << 20) % (margin + 1)
    lengths = lengths.at[donor].add(-shifted).at[taker].add(shifted)
    items = jnp.searchsorted(jnp.cumsum(lengths), jnp.arange(rows * top), side="right").astype(jnp.int32)
    table = items.reshape(top, rows).T
    table = table[jax.random.permutation(jax.random.fold_in(own, 1), rows)]
    rotation = jax.random.randint(jax.random.fold_in(own, 2), (rows, 1), 0, top)
    return jnp.take_along_axis(table, (jnp.arange(top)[None, :] + rotation) % top, axis=1)


def load_shares(number_of, total, bound, lean, full):
    weights = [(1 << 20) // math.isqrt(grade ** lean) + 1 for grade in range(1, number_of + 1)]
    largest = bound if full else min(bound, max(-(-total // number_of), total * weights[0] // sum(weights)))
    least = 1 if total - largest >= number_of - 1 else 0
    counts, surplus = [largest] + [least] * (number_of - 1), total - largest - least * (number_of - 1)
    while surplus > 0:
        candidates = [i for i in range(1, number_of) if counts[i] < largest] or [i for i in range(1, number_of) if counts[i] < bound]
        pool, remaining = sum([weights[i] for i in candidates]), surplus
        for i in candidates:
            addition = min(bound - counts[i], max(1, remaining * weights[i] // pool), surplus)
            counts[i] = counts[i] + addition
            surplus = surplus - addition
    return np.array(counts)


def scatter_about(stream_key, extent, width, bound, shards=(), kind=jnp.bfloat16):
    result = width * jax.random.normal(stream_key, extent, jnp.float32)
    if shards:
        result = result * shard_levels(stream_key, extent, shards, -0.22, 0.18)
    return jnp.clip(result, -bound, bound).astype(kind)


def setup_inputs(seed: int = 0) -> dict:
    key_list = jax.random.split(jax.random.key(seed), 6)
    flow_state = draw_flow_state(jax.random.fold_in(key_list[5], 71), 0)
    adjoint = scatter_about(key_list[1], (5, 64, ELEMENTS_FIRST, ELEMENTS_SECOND, ELEMENTS_THIRD), 1.0, 6.0, ((2, 8), (3, 4)), jnp.float32)
    displacement = draw_displacement(jax.random.fold_in(key_list[5], 71), 0)
    lattice_block_keys = jax.random.split(jax.random.fold_in(key_list[3], 1), N_PX * N_PY * DEVICE_VERTICES // DEVICE_VERTICES)
    lattice_block_turns = jax.random.permutation(jax.random.fold_in(key_list[3], 3), N_PX * N_PY * DEVICE_VERTICES // DEVICE_VERTICES)
    lattice_block = jax.vmap(lambda own, number: deal_out(jax.random.fold_in(key_list[3], 2), own, number, DEVICE_VERTICES, LATTICE_BLOCKS, 1, CAP, 2))(lattice_block_keys, lattice_block_turns).reshape((N_PX, N_PY, DEVICE_VERTICES, 1))
    lattice_coords = jnp.clip(0.02 + 0.96000002 * jax.random.uniform(key_list[4], (N_PX, N_PY, 3, DEVICE_VERTICES), jnp.float32) ** shard_levels(key_list[4], (N_PX, N_PY, 3, DEVICE_VERTICES), ((0, 8), (1, 4)), -0.2, 0.2), 0.02, 0.98)
    return {"flow_state": flow_state, "adjoint": adjoint, "displacement": displacement, "lattice_block": lattice_block, "lattice_coords": lattice_coords}


GAMMA_LESS = 0.4
DISSIPATION = 2.0
HIGHEST = lax.Precision.HIGHEST
COFACTOR_TERMS = [[((1, 1), (2, 2), (1, 2), (2, 1)), ((0, 2), (2, 1), (0, 1), (2, 2)), ((0, 1), (1, 2), (0, 2), (1, 1))], [((1, 2), (2, 0), (1, 0), (2, 2)), ((0, 0), (2, 2), (0, 2), (2, 0)), ((0, 2), (1, 0), (0, 0), (1, 2))], [((1, 0), (2, 1), (1, 1), (2, 0)), ((0, 1), (2, 0), (0, 0), (2, 1)), ((0, 0), (1, 1), (0, 1), (1, 0))]]

def gll_tables():
    points = [-1.0, -1.0 / math.sqrt(5.0), 1.0 / math.sqrt(5.0), 1.0]
    weights = np.array([1.0, 5.0, 5.0, 1.0]) / 6.0
    derivative = np.zeros((4, 4))
    for target in range(4):
        for source in range(4):
            if target == source:
                derivative[target, source] = sum((1.0 / (points[source] - points[member]) for member in range(4) if member != source))
            else:
                upper_part = 1.0
                lower_part = 1.0
                for member in range(4):
                    if member != source:
                        lower_part = lower_part * (points[source] - points[member])
                        if member != target:
                            upper_part = upper_part * (points[target] - points[member])
                derivative[target, source] = upper_part / lower_part
    return (points, weights, derivative)

def corner_table():
    points = gll_tables()[0]
    slope_table = np.zeros((3, 64, 8))
    for node_index in range(64):
        position_index = (node_index // 16, node_index // 4 % 4, node_index % 4)
        for corner in range(8):
            corner_signs = (2 * (corner // 4) - 1, 2 * (corner // 2 % 2) - 1, 2 * (corner % 2) - 1)
            for direction in range(3):
                factor = 1.0
                for member in range(3):
                    if member == direction:
                        factor = factor * 0.5 * corner_signs[member]
                    else:
                        factor = factor * 0.5 * (1.0 + corner_signs[member] * points[position_index[member]])
                slope_table[direction, node_index, corner] = factor
    return slope_table

def metric_terms(corners):
    slope_table = jnp.asarray(corner_table(), jnp.float32)
    jacobian = jnp.einsum('dnk,ckxyz->cdnxyz', slope_table, corners, precision=HIGHEST)
    entries = [[jacobian[member, target] + (0.5 if member == target else 0.0) for target in range(3)] for member in range(3)]
    row_list = []
    for direction in range(3):
        columns = []
        for component in range(3):
            first_a, first_b, second_a, second_b = COFACTOR_TERMS[direction][component]
            columns.append(entries[first_a[0]][first_a[1]] * entries[first_b[0]][first_b[1]] - entries[second_a[0]][second_a[1]] * entries[second_b[0]][second_b[1]])
        row_list.append(jnp.stack(columns))
    return jnp.stack(row_list)

def euler_flux(flow_state):
    density = flow_state[0]
    momentum = flow_state[1:4]
    energy = flow_state[4]
    velocity = momentum / density
    pressure = GAMMA_LESS * (energy - 0.5 * lax.optimization_barrier(jnp.sum(momentum * velocity, axis=0)))
    result_list = []
    for direction in range(3):
        columns = [momentum[direction]]
        for component in range(3):
            entry_value = momentum[component] * velocity[direction]
            if component == direction:
                entry_value = entry_value + pressure
            columns.append(entry_value)
        columns.append((energy + pressure) * velocity[direction])
        result_list.append(jnp.stack(columns))
    return jnp.stack(result_list)

def direction_slopes(adjoint):
    derivative = jnp.asarray(gll_tables()[2], jnp.float32)
    block_shape = adjoint.shape[2:]
    node_cube = adjoint.reshape((5, 4, 4, 4) + block_shape)
    first_dir = jnp.einsum('ma,fabcxyz->fmbcxyz', derivative, node_cube, precision=HIGHEST)
    second_dir = jnp.einsum('mb,fabcxyz->famcxyz', derivative, node_cube, precision=HIGHEST)
    third_dir = jnp.einsum('mc,fabcxyz->fabmxyz', derivative, node_cube, precision=HIGHEST)
    return jnp.stack([member.reshape((5, 64) + block_shape) for member in (first_dir, second_dir, third_dir)])

def volume_lagrangian(flow_state, adjugate, slopes):
    weights = gll_tables()[1]
    weight_table = jnp.asarray(np.kron(np.kron(weights, weights), weights), jnp.float32).reshape(1, 64, 1, 1, 1)
    fluxes = euler_flux(flow_state)
    running = jnp.zeros((), jnp.float32)
    for direction in range(3):
        contra = adjugate[direction, 0][None] * fluxes[0] + adjugate[direction, 1][None] * fluxes[1] + adjugate[direction, 2][None] * fluxes[2]
        running = running - jnp.sum(weight_table * slopes[direction] * contra)
    return running

def face_trace(nodal_field, direction, face_side):
    leading = nodal_field.shape[0]
    block_shape = nodal_field.shape[2:]
    node_cube = nodal_field.reshape((leading, 4, 4, 4) + block_shape)
    picked = lax.index_in_dim(node_cube, face_side, axis=1 + direction, keepdims=False)
    return picked.reshape((leading, 16) + block_shape)

def stacked_face(flow_state, adjoint, direction, face_side, layer_index):
    combined = jnp.concatenate([face_trace(flow_state, direction, face_side), face_trace(adjoint, direction, face_side)], axis=0)
    return lax.slice_in_dim(combined, layer_index, layer_index + 1, axis=2 + direction)

def face_lagrangian(minus_state, plus_state, adjoint_jump, face_normal):
    weights = gll_tables()[1]
    face_weights = jnp.asarray(np.kron(weights, weights), jnp.float32).reshape(1, 16, 1, 1, 1)
    minus_flux = euler_flux(minus_state)
    plus_flux = euler_flux(plus_state)
    average = 0.5 * (face_normal[0][None] * (minus_flux[0] + plus_flux[0]) + face_normal[1][None] * (minus_flux[1] + plus_flux[1]) + face_normal[2][None] * (minus_flux[2] + plus_flux[2]))
    length = jnp.sqrt(face_normal[0] * face_normal[0] + face_normal[1] * face_normal[1] + face_normal[2] * face_normal[2])
    numerical = average - 0.5 * DISSIPATION * length[None] * (plus_state - minus_state)
    return jnp.sum(face_weights * adjoint_jump * numerical)

def reflect_state(flow_state, face_normal):
    momentum = flow_state[1:4]
    projection = lax.optimization_barrier(jnp.sum(momentum * face_normal, axis=0)) / lax.optimization_barrier(jnp.sum(face_normal * face_normal, axis=0))
    return jnp.concatenate([flow_state[0:1], momentum - 2.0 * projection[None] * face_normal, flow_state[4:5]], axis=0)

def interface_sum(flow_state, adjoint, adjugate, direction, upper_face, lower_face, lower_mode, is_first, is_last):
    axis_here = 2 + direction
    layers = flow_state.shape[axis_here]
    top_state = face_trace(flow_state, direction, 3)
    top_adjoint = face_trace(adjoint, direction, 3)
    low_state = face_trace(flow_state, direction, 0)
    low_adjoint = face_trace(adjoint, direction, 0)
    top_normal = face_trace(adjugate[direction], direction, 3)
    last_top = lax.slice_in_dim(top_state, layers - 1, layers, axis=axis_here)
    upper_state = jnp.where(is_last, last_top, upper_face[0:5])
    next_state = jnp.concatenate([lax.slice_in_dim(low_state, 1, layers, axis=axis_here), upper_state], axis=axis_here)
    next_adjoint = jnp.concatenate([lax.slice_in_dim(low_adjoint, 1, layers, axis=axis_here), upper_face[5:10]], axis=axis_here)
    running = face_lagrangian(top_state, next_state, top_adjoint - next_adjoint, top_normal)
    if lower_mode != 'none':
        first_state = lax.slice_in_dim(low_state, 0, 1, axis=axis_here)
        first_adjoint = lax.slice_in_dim(low_adjoint, 0, 1, axis=axis_here)
        first_normal = lax.slice_in_dim(face_trace(adjugate[direction], direction, 0), 0, 1, axis=axis_here)
        mirrored = reflect_state(first_state, first_normal)
        if lower_mode == 'received':
            minus_state = jnp.where(is_first, mirrored, lower_face[0:5])
            used_normal = jnp.where(is_first, first_normal, lax.stop_gradient(first_normal))
            running = running + face_lagrangian(minus_state, first_state, lower_face[5:10] - first_adjoint, used_normal)
        else:
            running = running + jnp.where(is_first, 1.0, 0.0) * face_lagrangian(mirrored, first_state, -first_adjoint, first_normal)
    return running

def periodic_sum(flow_state, adjoint, adjugate):
    top_state = face_trace(flow_state, 2, 3)
    top_adjoint = face_trace(adjoint, 2, 3)
    next_state = jnp.roll(face_trace(flow_state, 2, 0), -1, axis=4)
    next_adjoint = jnp.roll(face_trace(adjoint, 2, 0), -1, axis=4)
    face_normal = face_trace(adjugate[2], 2, 3)
    return face_lagrangian(top_state, next_state, top_adjoint - next_adjoint, face_normal)

def make_lagrangian(adjoint, slopes, lower_x, lower_y, lower_modes, is_first, is_last):

    def lagrangian(flow_state, adjugate, upper_x, upper_y):
        running = volume_lagrangian(flow_state, adjugate, slopes)
        running = running + interface_sum(flow_state, adjoint, adjugate, 0, upper_x, lower_x, lower_modes[0], is_first, is_last)
        running = running + interface_sum(flow_state, adjoint, adjugate, 1, upper_y, lower_y, lower_modes[1], False, False)
        return running + periodic_sum(flow_state, adjoint, adjugate)
    return lagrangian

def bernstein(parameter, degree):
    orders = jnp.arange(degree + 1).astype(jnp.float32)[:, None]
    binomials = jnp.asarray(np.array([math.comb(degree, member) for member in range(degree + 1)]), jnp.float32)[:, None]
    return binomials * jnp.power(parameter[None, :], orders) * jnp.power(1.0 - parameter[None, :], degree - orders)

def reference(flow_state, adjoint, displacement, lattice_block, lattice_coords):
    global_x = jnp.arange(ELEMENTS_FIRST + 1, dtype=jnp.int32)
    owner_x = jnp.minimum(global_x // DEVICE_ELEMS_X, ELEMENTS_FIRST // DEVICE_ELEMS_X - 1)
    xindex = (owner_x * (DEVICE_ELEMS_X + 1) + global_x - owner_x * DEVICE_ELEMS_X).astype(jnp.int32)
    global_y = jnp.arange(ELEMENTS_SECOND, dtype=jnp.int32)
    owner_y = global_y // DEVICE_ELEMS_Y
    yindex = (owner_y * (DEVICE_ELEMS_Y + 1) + global_y - owner_y * DEVICE_ELEMS_Y).astype(jnp.int32)
    vertices = jnp.take(jnp.take(displacement, xindex, axis=1), yindex, axis=2)

    def layer_update(vertex_sensitivity_sum, layer_index):
        here_state = lax.dynamic_slice_in_dim(flow_state, layer_index, 1, axis=2)
        here_adjoint = lax.dynamic_slice_in_dim(adjoint, layer_index, 1, axis=2)
        above_index = jnp.minimum(layer_index + 1, ELEMENTS_FIRST - 1)
        below_index = jnp.maximum(layer_index - 1, 0)
        above_keep = jnp.where(layer_index < ELEMENTS_FIRST - 1, 1.0, 0.0).astype(jnp.float32)
        below_keep = jnp.where(layer_index > 0, 1.0, 0.0).astype(jnp.float32)
        above_state = lax.dynamic_slice_in_dim(flow_state, above_index, 1, axis=2)
        above_adjoint = lax.dynamic_slice_in_dim(adjoint, above_index, 1, axis=2)
        below_state = lax.dynamic_slice_in_dim(flow_state, below_index, 1, axis=2)
        below_adjoint = lax.dynamic_slice_in_dim(adjoint, below_index, 1, axis=2)
        upper_x = stacked_face(above_state, above_adjoint, 0, 0, 0) * above_keep
        lower_x = stacked_face(below_state, below_adjoint, 0, 3, 0) * below_keep
        upper_y = stacked_face(here_state, here_adjoint, 1, 0, 0)
        lower_y = stacked_face(here_state, here_adjoint, 1, 3, ELEMENTS_SECOND - 1)
        layers_two = lax.dynamic_slice_in_dim(vertices, layer_index, 2, axis=1)
        corners = jnp.stack([jnp.roll(jnp.roll(layers_two[:, corner // 4:corner // 4 + 1], -(corner // 2 % 2), axis=2), -(corner % 2), axis=3) for corner in range(8)], axis=1)
        adjugate, metric_pull = jax.vjp(metric_terms, corners)
        slopes = direction_slopes(here_adjoint)
        lagrangian = make_lagrangian(here_adjoint, slopes, lower_x, lower_y, ('received', 'received'), layer_index == 0, layer_index == ELEMENTS_FIRST - 1)
        lagrange_value, pullback = jax.vjp(lagrangian, here_state, adjugate, upper_x, upper_y)
        grad_state, grad_adjugate, unused_x, unused_y = pullback(jnp.ones((), jnp.float32))
        grad_corners, = metric_pull(grad_adjugate)
        pieces = [jnp.roll(jnp.roll(grad_corners[:, corner], corner // 2 % 2, axis=2), corner % 2, axis=3) for corner in range(8)]
        low_add = pieces[0] + pieces[1] + pieces[2] + pieces[3]
        high_add = pieces[4] + pieces[5] + pieces[6] + pieces[7]
        current = lax.dynamic_slice_in_dim(vertex_sensitivity_sum, layer_index, 2, axis=1)
        vertex_sensitivity_sum = lax.dynamic_update_slice_in_dim(vertex_sensitivity_sum, current + jnp.concatenate([low_add, high_add], axis=1), layer_index, axis=1)
        return (vertex_sensitivity_sum, grad_state[:, :, 0])
    vertex_sensitivity_sum, layer_gradients = lax.scan(layer_update, jnp.zeros((3, ELEMENTS_FIRST + 1, ELEMENTS_SECOND, ELEMENTS_THIRD), jnp.float32), jnp.arange(ELEMENTS_FIRST, dtype=jnp.int32))
    adjoint_residual = jnp.transpose(layer_gradients, (1, 2, 0, 3, 4))
    owned_vertex_sensitivity = vertex_sensitivity_sum[:, 0:ELEMENTS_FIRST]
    row_sensitivity = jnp.transpose(owned_vertex_sensitivity.reshape(3, N_PX, DEVICE_ELEMS_X, N_PY, DEVICE_ELEMS_Y, ELEMENTS_THIRD), (1, 3, 0, 2, 4, 5)).reshape(LATTICE_BLOCKS, 3, DEVICE_VERTICES)
    coords = lattice_coords.reshape(LATTICE_BLOCKS, 3, DEVICE_VERTICES)
    blocks = lattice_block.reshape(LATTICE_BLOCKS, DEVICE_VERTICES)

    def group_step(lattice_total, inputs):
        sens_rows, coord_rows, block_rows = inputs
        along_u = bernstein(coord_rows[0], LU - 1)
        along_v = bernstein(coord_rows[1], LV - 1)
        along_w = bernstein(coord_rows[2], LW - 1)
        outer_product = sens_rows[:, None, None, None, :] * along_u[None, :, None, None, :] * along_v[None, None, :, None, :] * along_w[None, None, None, :, :]
        flattened = jnp.transpose(outer_product.reshape(3 * LPTS, DEVICE_VERTICES))
        return (lattice_total + jax.ops.segment_sum(flattened, block_rows, num_segments=LATTICE_BLOCKS), None)
    lattice_total, unused = lax.scan(group_step, jnp.zeros((LATTICE_BLOCKS, 3 * LPTS), jnp.float32), (row_sensitivity, coords, blocks))
    lattice_grad = lattice_total.reshape(N_PX, N_PY, 3, LPTS)
    return (adjoint_residual, owned_vertex_sensitivity, lattice_grad)
```

```python
import functools
import math

import jax
import jax.numpy as jnp
import numpy as np
from jax import lax
from jax.experimental import pallas as pl
from jax.experimental.pallas import tpu as pltpu
from jax.sharding import PartitionSpec as P

LU = 12
LV = 12
LW = 6
HIGHEST = lax.Precision.HIGHEST
F32 = jnp.float32
POINTS = [-1.0, -1.0 / math.sqrt(5.0), 1.0 / math.sqrt(5.0), 1.0]
WEIGHTS = [1.0 / 6.0, 5.0 / 6.0, 5.0 / 6.0, 1.0 / 6.0]
UPPER = [0.5 * (1.0 + point) for point in POINTS]


def derivative_matrix():
    matrix = np.zeros((4, 4))
    for target in range(4):
        for source in range(4):
            others = [m for m in range(4) if m != source]
            if target == source:
                matrix[target, source] = sum(1.0 / (POINTS[source] - POINTS[m]) for m in others)
            else:
                upper = np.prod([POINTS[target] - POINTS[m] for m in others if m != target])
                lower = np.prod([POINTS[source] - POINTS[m] for m in others])
                matrix[target, source] = upper / lower
    return matrix


DM = derivative_matrix()


def line_slopes(line, scale):
    e0 = line[0] + line[3]
    o0 = line[0] - line[3]
    e1 = line[1] + line[2]
    o1 = line[1] - line[2]
    even = e0 - e1
    out = [None] * 4
    for m in range(2):
        half = 0.5 * scale[m]
        p0 = float(half * (DM[m, 0] - DM[m, 3]))
        p1 = float(half * (DM[m, 1] - DM[m, 2]))
        k = float(half * (DM[m, 0] + DM[m, 3]))
        odd_part = p0 * o0 + p1 * o1
        even_part = k * even
        out[m] = odd_part + even_part
        out[3 - m] = odd_part - even_part
    return out


def spread(low, high):
    step = high - low
    return [low, low + float(UPPER[1]) * step, low + float(UPPER[2]) * step, high]


def gather_back(g):
    middle = float(UPPER[1]) * g[1] + float(UPPER[2]) * g[2]
    return (g[0] + g[1] + g[2] - middle, g[3] + middle)


def cross(x, y):
    return [x[1] * y[2] - x[2] * y[1], x[2] * y[0] - x[0] * y[2], x[0] * y[1] - x[1] * y[0]]


def dot3(x, y):
    return x[0] * y[0] + x[1] * y[1] + x[2] * y[2]


def add(x, y):
    return y if x is None else x + y


def add3(x, y):
    return y if x is None else [x[i] + y[i] for i in range(3)]


def primitives(u):
    inverse = 1.0 / u[0]
    v = [u[1] * inverse, u[2] * inverse, u[3] * inverse]
    mv = u[1] * v[0] + u[2] * v[1] + u[3] * v[2]
    p = 0.4 * u[4] - 0.2 * mv
    return inverse, v, mv * inverse, p, u[4] + p


class Node:
    def __init__(self, u):
        self.inverse, self.v, self.v2, self.p, self.ep = primitives(u)
        self.big = [u[0], u[1], u[2], u[3], self.ep]
        self.w = [None] * 5
        self.pb = None
        self.b = None

    def work(self, s):
        return sum((s[f] * self.big[f] for f in range(1, 5)), s[0] * self.big[0])

    def volume(self, adj, s, vn):
        back = []
        for d in range(3):
            k = self.work(s[d])
            for f in range(5):
                self.w[f] = add(self.w[f], vn[d] * s[d][f])
            self.pb = add(self.pb, dot3(adj[d], s[d][1:4]))
            self.b = add3(self.b, [adj[d][c] * k for c in range(3)])
            back.append([self.v[c] * k + self.p * s[d][1 + c] for c in range(3)])
        self.pb = self.pb + self.w[4]
        return back

    def face(self, n, vn, jump, sigma):
        k = self.work(jump)
        square = dot3(n, n)
        root = lax.rsqrt(square)
        twice = 2.0 * root
        length = twice * square
        if isinstance(sigma, int) and sigma == 1:
            cf = vn + length
        elif isinstance(sigma, int):
            cf = vn - length
            twice = -twice
        else:
            cf = vn + sigma * length
            twice = sigma * twice
        q = k - jump[4] * self.p
        along = twice * q
        for f in range(5):
            self.w[f] = add(self.w[f], cf * jump[f])
        self.pb = add(self.pb, dot3(n, jump[1:4]) + vn * jump[4])
        self.b = add3(self.b, [n[c] * k for c in range(3)])
        return [self.v[c] * k + self.p * jump[1 + c] + n[c] * along for c in range(3)]

    def gradient(self):
        pb4 = 0.4 * self.pb
        rb = [self.b[c] * self.inverse for c in range(3)]
        out = [self.w[0] - dot3(self.v, rb) + (0.5 * pb4) * self.v2]
        for c in range(3):
            out.append(self.w[1 + c] + rb[c] - pb4 * self.v[c])
        out.append(self.w[4] + pb4)
        return out


def corner(disp_ref, c, e1, e2, e3):
    window = disp_ref[c, e1, e2 : e2 + 8, :]
    return pltpu.roll(window, 127, 1) if e3 else window


def volume_kernel(u_ref, lam_ref, disp_ref, yup_ref, ydn_ref, grad_ref, g_ref, j0t, j1t, j2t, j0b, j1b, j2b, s1, s2, yj):
    a = pl.program_id(0)

    @pl.when(a == 0)
    def _():
        for c in range(3):
            x = [[[corner(disp_ref, c, e1, e2, e3) for e3 in range(2)] for e2 in range(2)] for e1 in range(2)]
            for d in range(3):
                ends = []
                for i in range(2):
                    pair = []
                    for j in range(2):
                        low = [(0, i, j), (i, 0, j), (i, j, 0)][d]
                        high = [(1, i, j), (i, 1, j), (i, j, 1)][d]
                        half = 0.5 * (x[high[0]][high[1]][high[2]] - x[low[0]][low[1]][low[2]])
                        pair.append(half + 0.5 if c == d else half)
                    ends.append(spread(pair[0], pair[1]))
                for j in range(4):
                    values = spread(ends[0][j], ends[1][j])
                    for i in range(4):
                        [j0t, j1t, j2t][d][i, j, c] = values[i]
        j0b[...] = jnp.zeros_like(j0b)
        for f in range(5):
            for b in range(4):
                for c in range(4):
                    weight = -WEIGHTS[b] * WEIGHTS[c]
                    line = [lam_ref[f, 16 * i + 4 * b + c] for i in range(4)]
                    out = line_slopes(line, [weight] * 4)
                    for i in range(4):
                        s1[i, 4 * b + c, f] = out[i]

    wa = jnp.where((a == 0) | (a == 3), F32(WEIGHTS[0]), F32(WEIGHTS[1]))
    rows = lax.broadcasted_iota(jnp.int32, (8, 128), 0)
    first_row = rows == 0
    last_row = rows == 7
    base = a * 16
    for f in range(5):
        for c in range(4):
            line = [lam_ref[f, base + 4 * b + c] for b in range(4)]
            out = line_slopes(line, [-WEIGHTS[b] * WEIGHTS[c] for b in range(4)])
            for b in range(4):
                s2[4 * b + c, f] = out[b]
            half = float(0.5 * WEIGHTS[c])
            above = yup_ref[pl.ds(f * 16 + a * 4 + c, 1), :]
            below = ydn_ref[pl.ds(f * 16 + a * 4 + c, 1), :]
            plus = jnp.where(last_row, jnp.broadcast_to(above, (8, 128)), pltpu.roll(line[0], 7, 0))
            top = half * (line[3] - plus)
            bottom = half * (jnp.broadcast_to(below, (8, 128)) - line[0])
            yj[1, c, f] = top
            yj[0, c, f] = jnp.where(first_row, bottom, pltpu.roll(top, 1, 0))

    for b in range(4):
        slopes3 = []
        ztop = []
        zbot = []
        half = float(0.5 * WEIGHTS[b])
        for f in range(5):
            line = [lam_ref[f, base + 4 * b + c] for c in range(4)]
            slopes3.append(line_slopes(line, [-WEIGHTS[b] * WEIGHTS[c] for c in range(4)]))
            top = half * (line[3] - pltpu.roll(line[0], 127, 1))
            ztop.append(top)
            zbot.append(pltpu.roll(top, 1, 1))
        back2 = None
        col2 = [j2t[a, b, k] for k in range(3)]
        for c in range(4):
            n = 4 * b + c
            node = Node([u_ref[f, n] for f in range(5)])
            col0 = [j0t[b, c, k] for k in range(3)]
            col1 = [j1t[a, c, k] for k in range(3)]
            adj = [cross(col1, col2), cross(col2, col0), cross(col0, col1)]
            s = [[s1[a, n, f] for f in range(5)], [s2[n, f] for f in range(5)], [slopes3[f][c] for f in range(5)]]
            vn = [dot3(adj[d], node.v) for d in range(3)]
            back = node.volume(adj, s, vn)
            if b == 0:
                back[1] = add3(back[1], node.face(adj[1], vn[1], [yj[0, c, f] for f in range(5)], -1))
            if b == 3:
                back[1] = add3(back[1], node.face(adj[1], vn[1], [yj[1, c, f] for f in range(5)], 1))
            if c == 0:
                back[2] = add3(back[2], node.face(adj[2], vn[2], zbot, -1))
            if c == 3:
                back[2] = add3(back[2], node.face(adj[2], vn[2], ztop, 1))
            grads = node.gradient()
            for f in range(5):
                grad_ref[f, n] = wa * grads[f]
            back0 = add3(cross(back[1], col2), cross(col1, back[2]))
            back1 = add3(cross(col2, back[0]), cross(back[2], col0))
            back2 = add3(back2, add3(cross(back[0], col1), cross(col0, back[1])))
            for k in range(3):
                j0b[b, c, k] = j0b[b, c, k] + wa * back0[k]
                j1b[a, c, k] = back1[k] if b == 0 else j1b[a, c, k] + back1[k]
        for k in range(3):
            j2b[a, b, k] = back2[k]

    @pl.when(a == 3)
    def _():
        for c in range(3):
            gx = [[[None, None], [None, None]], [[None, None], [None, None]]]
            for d in range(3):
                table = [j0b, j1b, j2b][d]
                ends = [[], []]
                for i in range(4):
                    low, high = gather_back([table[i, j, c] for j in range(4)])
                    if d:
                        low, high = WEIGHTS[i] * low, WEIGHTS[i] * high
                    ends[0].append(low)
                    ends[1].append(high)
                for j in range(2):
                    pair = gather_back(ends[j])
                    for i in range(2):
                        half = 0.5 * pair[i]
                        low = [(0, i, j), (i, 0, j), (i, j, 0)][d]
                        high = [(1, i, j), (i, 1, j), (i, j, 1)][d]
                        gx[high[0]][high[1]][high[2]] = add(gx[high[0]][high[1]][high[2]], half)
                        gx[low[0]][low[1]][low[2]] = add(gx[low[0]][low[1]][low[2]], -half)
            for e1 in range(2):
                for e2 in range(2):
                    g_ref[e1, c, e2] = gx[e1][e2][0] + pltpu.roll(gx[e1][e2][1], 1, 1)


def face_kernel(flags_ref, u_ref, lam_ref, disp_ref, lower_ref, upper_ref, g_ref, grad_in_ref, grad_ref, part_ref, row_ref):
    side = pl.program_id(0)
    is_first = flags_ref[0] == 1
    is_last = flags_ref[1] == 1

    def run(received_ref, wall, scale, sigma):
        col1 = [[None] * 3 for _ in range(4)]
        col2 = [[None] * 3 for _ in range(4)]
        for k in range(3):
            x = [[corner(disp_ref, k, side, e2, e3) for e3 in range(2)] for e2 in range(2)]
            along1 = spread(0.5 * (x[1][0] - x[0][0]), 0.5 * (x[1][1] - x[0][1]))
            along2 = spread(0.5 * (x[0][1] - x[0][0]), 0.5 * (x[1][1] - x[1][0]))
            for i in range(4):
                col1[i][k] = along1[i] + 0.5 if k == 1 else along1[i]
                col2[i][k] = along2[i] + 0.5 if k == 2 else along2[i]
        back1 = [None] * 4
        back2 = [None] * 4
        for b in range(4):
            for c in range(4):
                n = 4 * b + c
                weight = float(WEIGHTS[b] * WEIGHTS[c])
                u = [u_ref[f, n] for f in range(5)]
                own = [lam_ref[f, n] for f in range(5)]
                normal = cross(col1[c], col2[b])
                if wall:
                    inverse, v, v2, p, ep = primitives(u)
                    vn = dot3(normal, v)
                    m = u[1:4]
                    jump = [-weight * own[f] for f in range(1, 4)]
                    square = dot3(normal, normal)
                    root = lax.rsqrt(square)
                    rate = vn * (root * root)
                    q = u[0] * vn
                    level = dot3(jump, normal)
                    slope = 2.0 * (rate - root)
                    phi = q * (rate - 2.0 * root) + p
                    lk = level * slope
                    along = lk * q * (root * root)
                    grads = [level * (0.2 * v2 - rate * vn)]
                    for k in range(3):
                        grads.append(lk * normal[k] - (0.4 * level) * v[k])
                    grads.append(0.4 * level)
                    back = [jump[k] * phi + lk * m[k] - along * normal[k] for k in range(3)]
                else:
                    node = Node(u)
                    vn = dot3(normal, node.v)
                    factor = scale * weight
                    jump = [factor * (own[f] - received_ref[f, n]) for f in range(5)]
                    back = node.face(normal, vn, jump, sigma)
                    grads = node.gradient()
                for f in range(5):
                    grad_ref[f, n] = grad_in_ref[f, n] + grads[f]
                back1[c] = add3(back1[c], cross(col2[b], back))
                back2[b] = add3(back2[b], cross(back, col1[c]))
        for k in range(3):
            low1, high1 = gather_back([back1[i][k] for i in range(4)])
            low2, high2 = gather_back([back2[i][k] for i in range(4)])
            gx = [[-0.5 * (low1 + low2), 0.5 * (low2 - high1)], [0.5 * (low1 - high2), 0.5 * (high1 + high2)]]
            near = g_ref[0, k, 0] + gx[0][0] + pltpu.roll(gx[0][1], 1, 1)
            far = g_ref[0, k, 1] + gx[1][0] + pltpu.roll(gx[1][1], 1, 1)
            rows = lax.broadcasted_iota(jnp.int32, (8, 128), 0)
            part_ref[0, k] = near + jnp.where(rows == 0, 0.0, pltpu.roll(far, 1, 0))
            row_ref[0, k : k + 1, :] = far[7:8, :]

    @pl.when((side == 0) & is_first)
    def _():
        run(None, True, None, None)

    @pl.when((side == 0) & jnp.logical_not(is_first))
    def _():
        run(lower_ref, False, -0.5, -1)

    @pl.when(side == 1)
    def _():
        run(upper_ref, False, jnp.where(is_last, F32(1.0), F32(0.5)), jnp.where(is_last, F32(0.0), F32(1.0)))


def volume_call(u, lam, disp, yup, ydn):
    tile = (8, 128)
    whole = lambda shape: pl.BlockSpec(shape, lambda a: (0,) * len(shape))
    return pl.pallas_call(
        volume_kernel,
        grid=(4,),
        in_specs=[
            pl.BlockSpec((5, 16) + tile, lambda a: (0, a, 0, 0)),
            whole(lam.shape),
            whole(disp.shape),
            whole(yup.shape),
            whole(ydn.shape),
        ],
        out_specs=[
            pl.BlockSpec((5, 16) + tile, lambda a: (0, a, 0, 0)),
            whole((2, 3, 2) + tile),
        ],
        out_shape=[
            jax.ShapeDtypeStruct((5, 64) + tile, F32),
            jax.ShapeDtypeStruct((2, 3, 2) + tile, F32),
        ],
        scratch_shapes=[pltpu.VMEM((4, 4, 3) + tile, F32)] * 6
        + [
            pltpu.VMEM((4, 16, 5) + tile, F32),
            pltpu.VMEM((16, 5) + tile, F32),
            pltpu.VMEM((2, 4, 5) + tile, F32),
        ],
        name="volume",
    )(u, lam, disp, yup, ydn)


def face_call(flags, u, lam, disp, lower, upper, g, grad):
    tile = (8, 128)
    whole = lambda shape: pl.BlockSpec(shape, lambda a: (0,) * len(shape))
    side_block = pl.BlockSpec((5, 16) + tile, lambda a: (0, 3 * a, 0, 0))
    return pl.pallas_call(
        face_kernel,
        grid=(2,),
        in_specs=[
            pl.BlockSpec(memory_space=pltpu.SMEM),
            side_block,
            side_block,
            whole(disp.shape),
            whole(lower.shape),
            whole(upper.shape),
            pl.BlockSpec((1, 3, 2) + tile, lambda a: (a, 0, 0, 0, 0)),
            side_block,
        ],
        out_specs=[
            side_block,
            pl.BlockSpec((1, 3) + tile, lambda a: (a, 0, 0, 0)),
            pl.BlockSpec((1, 3, 128), lambda a: (a, 0, 0)),
        ],
        out_shape=[
            jax.ShapeDtypeStruct((5, 64) + tile, F32),
            jax.ShapeDtypeStruct((2, 3) + tile, F32),
            jax.ShapeDtypeStruct((2, 3, 128), F32),
        ],
        input_output_aliases={7: 0},
        name="faces",
    )(flags, u, lam, disp, lower, upper, g, grad)


def bernstein(parameter, degree):
    orders = jnp.arange(degree + 1).astype(jnp.float32)[:, None]
    binomials = jnp.asarray(
        np.array([math.comb(degree, member) for member in range(degree + 1)]), jnp.float32
    )[:, None]
    return (
        binomials
        * jnp.power(parameter[None, :], orders)
        * jnp.power(1.0 - parameter[None, :], degree - orders)
    )


def bernstein_rows(sensitivity, coords):
    row_count = sensitivity.shape[1]
    along_u = bernstein(coords[0], LU - 1)
    along_v = bernstein(coords[1], LV - 1)
    along_w = bernstein(coords[2], LW - 1)
    inner_rows = (
        sensitivity[:, None, None, :] * along_v[None, :, None, :] * along_w[None, None, :, :]
    ).reshape(3 * LV * LW, row_count)
    return (along_u, inner_rows)


def shift_px(payload, step):
    length = lax.axis_size("px")
    pairs = [(i, i + step) for i in range(length) if 0 <= i + step < length]
    return lax.ppermute(payload, "px", pairs)


def shift_py(payload, step):
    length = lax.axis_size("py")
    return lax.ppermute(payload, "py", [(i, (i + step) % length) for i in range(length)])


def per_device(flow_state, adjoint, displacement, lattice_block, lattice_coords):
    u = flow_state.reshape(5, 64, 8, 128)
    lam = adjoint.reshape(5, 64, 8, 128)
    index = lax.axis_index("px")
    flags = jnp.stack([index == 0, index == lax.axis_size("px") - 1]).astype(jnp.int32)
    upper = shift_px(lam[:, 0:16], -1)
    lower = shift_px(lam[:, 48:64], 1)
    cube = lam.reshape(5, 4, 4, 4, 8, 128)
    yup = shift_py(cube[:, :, 0, :, 0, :].reshape(80, 128), -1)
    ydn = shift_py(cube[:, :, 3, :, 7, :].reshape(80, 128), 1)
    grad, g = volume_call(u, lam, displacement, yup, ydn)
    grad, part, rows = face_call(flags, u, lam, displacement, lower, upper, g, grad)
    rows = shift_py(rows, 1)
    part = part.at[:, :, 0, :].add(rows)
    owned = part[0] + shift_px(part[1], 1)
    owned_vertex_sensitivity = owned.reshape(3, 1, 8, 128)
    sensitivity = owned.reshape(3, -1)
    row_count = sensitivity.shape[1]
    coords = lattice_coords.reshape(3, row_count)
    block_ids = lattice_block.reshape(row_count)
    device_count = lax.axis_size("px") * lax.axis_size("py")
    capacity = max(2, 2 * row_count // device_count)
    block_range = jnp.arange(device_count, dtype=jnp.int32)
    matches = (block_ids[:, None] == block_range[None, :]).astype(jnp.int32)
    running_counts = jnp.cumsum(matches, axis=0)
    slot_ranks = jnp.sum(matches * (running_counts - 1), axis=1)
    targets = block_ids * capacity + slot_ranks
    slot_range = jnp.arange(device_count * capacity, dtype=jnp.int32)
    placement = (targets[:, None] == slot_range[None, :]).astype(jnp.float32)
    payload = jnp.concatenate([sensitivity, coords], axis=0)
    buffer = jnp.dot(payload, placement, precision=HIGHEST, preferred_element_type=jnp.float32)
    received = lax.all_to_all(buffer, ("px", "py"), split_axis=1, concat_axis=1, tiled=True)
    along_u, inner_rows = bernstein_rows(received[0:3], received[3:6])
    product = jnp.einsum("ar,jr->aj", along_u, inner_rows, precision=HIGHEST)
    block_grad = jnp.transpose(product.reshape(LU, 3, LV * LW), (1, 0, 2)).reshape(3, LU * LV * LW)
    lattice_grad = block_grad.reshape(1, 1, 3, LU * LV * LW)
    return (grad.reshape(5, 64, 1, 8, 128), owned_vertex_sensitivity, lattice_grad)


def solution(mesh):
    in_specs = (
        P(None, None, "px", "py", None),
        P(None, None, "px", "py", None),
        P(None, "px", "py", None),
        P("px", "py", None, None),
        P("px", "py", None, None),
    )
    out_specs = (
        P(None, None, "px", "py", None),
        P(None, "px", "py", None),
        P("px", "py", None, None),
    )
    return jax.shard_map(
        per_device, mesh=mesh, in_specs=in_specs, out_specs=out_specs, check_vma=False
    )
```

```python
import functools
import math

import jax
import jax.numpy as jnp
import numpy as np
from jax import lax
from jax.experimental import pallas as pl
from jax.experimental.pallas import tpu as pltpu
from jax.sharding import PartitionSpec as P

LU = 12
LV = 12
LW = 6
F32 = jnp.float32
POINTS = [-1.0, -1.0 / math.sqrt(5.0), 1.0 / math.sqrt(5.0), 1.0]
WEIGHTS = [1.0 / 6.0, 5.0 / 6.0, 5.0 / 6.0, 1.0 / 6.0]
UPPER = [0.5 * (1.0 + point) for point in POINTS]


def derivative_matrix():
    matrix = np.zeros((4, 4))
    for target in range(4):
        for source in range(4):
            others = [m for m in range(4) if m != source]
            if target == source:
                matrix[target, source] = sum(1.0 / (POINTS[source] - POINTS[m]) for m in others)
            else:
                upper = np.prod([POINTS[target] - POINTS[m] for m in others if m != target])
                lower = np.prod([POINTS[source] - POINTS[m] for m in others])
                matrix[target, source] = upper / lower
    return matrix


DM = derivative_matrix()


def line_slopes(line, scale):
    e0 = line[0] + line[3]
    o0 = line[0] - line[3]
    e1 = line[1] + line[2]
    o1 = line[1] - line[2]
    even = e0 - e1
    out = [None] * 4
    for m in range(2):
        half = 0.5 * scale[m]
        p0 = float(half * (DM[m, 0] - DM[m, 3]))
        p1 = float(half * (DM[m, 1] - DM[m, 2]))
        k = float(half * (DM[m, 0] + DM[m, 3]))
        odd_part = p0 * o0 + p1 * o1
        even_part = k * even
        out[m] = odd_part + even_part
        out[3 - m] = odd_part - even_part
    return out


def spread(low, high):
    step = high - low
    return [low, low + float(UPPER[1]) * step, low + float(UPPER[2]) * step, high]


def gather_back(g):
    middle = float(UPPER[1]) * g[1] + float(UPPER[2]) * g[2]
    return (g[0] + g[1] + g[2] - middle, g[3] + middle)


def cross(x, y):
    return [x[1] * y[2] - x[2] * y[1], x[2] * y[0] - x[0] * y[2], x[0] * y[1] - x[1] * y[0]]


def dot3(x, y):
    return x[0] * y[0] + x[1] * y[1] + x[2] * y[2]


def add(x, y):
    return y if x is None else x + y


def add3(x, y):
    return y if x is None else [x[i] + y[i] for i in range(3)]


def primitives(u):
    inverse = 1.0 / u[0]
    v = [u[1] * inverse, u[2] * inverse, u[3] * inverse]
    mv = u[1] * v[0] + u[2] * v[1] + u[3] * v[2]
    p = 0.4 * u[4] - 0.2 * mv
    return inverse, v, mv * inverse, p, u[4] + p


class Node:
    def __init__(self, u):
        self.inverse, self.v, self.v2, self.p, self.ep = primitives(u)
        self.big = [u[0], u[1], u[2], u[3], self.ep]
        self.w = [None] * 5
        self.pb = None
        self.b = None

    def work(self, s):
        return sum((s[f] * self.big[f] for f in range(1, 5)), s[0] * self.big[0])

    def volume(self, adj, s, vn):
        back = []
        for d in range(3):
            k = self.work(s[d])
            for f in range(5):
                self.w[f] = add(self.w[f], vn[d] * s[d][f])
            self.pb = add(self.pb, dot3(adj[d], s[d][1:4]))
            self.b = add3(self.b, [adj[d][c] * k for c in range(3)])
            back.append([self.v[c] * k + self.p * s[d][1 + c] for c in range(3)])
        self.pb = self.pb + self.w[4]
        return back

    def face(self, n, vn, jump, sigma):
        k = self.work(jump)
        square = dot3(n, n)
        root = lax.rsqrt(square)
        twice = 2.0 * root
        length = twice * square
        if isinstance(sigma, int) and sigma == 1:
            cf = vn + length
        elif isinstance(sigma, int):
            cf = vn - length
            twice = -twice
        else:
            cf = vn + sigma * length
            twice = sigma * twice
        q = k - jump[4] * self.p
        along = twice * q
        for f in range(5):
            self.w[f] = add(self.w[f], cf * jump[f])
        self.pb = add(self.pb, dot3(n, jump[1:4]) + vn * jump[4])
        self.b = add3(self.b, [n[c] * k for c in range(3)])
        return [self.v[c] * k + self.p * jump[1 + c] + n[c] * along for c in range(3)]

    def gradient(self):
        pb4 = 0.4 * self.pb
        rb = [self.b[c] * self.inverse for c in range(3)]
        out = [self.w[0] - dot3(self.v, rb) + (0.5 * pb4) * self.v2]
        for c in range(3):
            out.append(self.w[1 + c] + rb[c] - pb4 * self.v[c])
        out.append(self.w[4] + pb4)
        return out


def corner(disp_ref, c, e1, e2, e3):
    window = disp_ref[c, e1, e2 : e2 + 8, :]
    return pltpu.roll(window, 127, 1) if e3 else window


def volume_kernel(u_ref, lam_ref, disp_ref, yup_ref, ydn_ref, grad_ref, g_ref, j0t, j1t, j2t, j0b, j1b, j2b, s1, s2, yj):
    a = pl.program_id(0)

    @pl.when(a == 0)
    def _():
        for c in range(3):
            x = [[[corner(disp_ref, c, e1, e2, e3) for e3 in range(2)] for e2 in range(2)] for e1 in range(2)]
            for d in range(3):
                ends = []
                for i in range(2):
                    pair = []
                    for j in range(2):
                        low = [(0, i, j), (i, 0, j), (i, j, 0)][d]
                        high = [(1, i, j), (i, 1, j), (i, j, 1)][d]
                        half = 0.5 * (x[high[0]][high[1]][high[2]] - x[low[0]][low[1]][low[2]])
                        pair.append(half + 0.5 if c == d else half)
                    ends.append(spread(pair[0], pair[1]))
                for j in range(4):
                    values = spread(ends[0][j], ends[1][j])
                    for i in range(4):
                        [j0t, j1t, j2t][d][i, j, c] = values[i]
        j0b[...] = jnp.zeros_like(j0b)
        for f in range(5):
            for b in range(4):
                for c in range(4):
                    weight = -WEIGHTS[b] * WEIGHTS[c]
                    line = [lam_ref[f, 16 * i + 4 * b + c] for i in range(4)]
                    out = line_slopes(line, [weight] * 4)
                    for i in range(4):
                        s1[i, 4 * b + c, f] = out[i]

    wa = jnp.where((a == 0) | (a == 3), F32(WEIGHTS[0]), F32(WEIGHTS[1]))
    rows = lax.broadcasted_iota(jnp.int32, (8, 128), 0)
    first_row = rows == 0
    last_row = rows == 7
    base = a * 16
    for f in range(5):
        for c in range(4):
            line = [lam_ref[f, base + 4 * b + c] for b in range(4)]
            out = line_slopes(line, [-WEIGHTS[b] * WEIGHTS[c] for b in range(4)])
            for b in range(4):
                s2[4 * b + c, f] = out[b]
            half = float(0.5 * WEIGHTS[c])
            above = yup_ref[pl.ds(f * 16 + a * 4 + c, 1), :]
            below = ydn_ref[pl.ds(f * 16 + a * 4 + c, 1), :]
            plus = jnp.where(last_row, jnp.broadcast_to(above, (8, 128)), pltpu.roll(line[0], 7, 0))
            top = half * (line[3] - plus)
            bottom = half * (jnp.broadcast_to(below, (8, 128)) - line[0])
            yj[1, c, f] = top
            yj[0, c, f] = jnp.where(first_row, bottom, pltpu.roll(top, 1, 0))

    for b in range(4):
        slopes3 = []
        ztop = []
        zbot = []
        half = float(0.5 * WEIGHTS[b])
        for f in range(5):
            line = [lam_ref[f, base + 4 * b + c] for c in range(4)]
            slopes3.append(line_slopes(line, [-WEIGHTS[b] * WEIGHTS[c] for c in range(4)]))
            top = half * (line[3] - pltpu.roll(line[0], 127, 1))
            ztop.append(top)
            zbot.append(pltpu.roll(top, 1, 1))
        back2 = None
        col2 = [j2t[a, b, k] for k in range(3)]
        for c in range(4):
            n = 4 * b + c
            node = Node([u_ref[f, n] for f in range(5)])
            col0 = [j0t[b, c, k] for k in range(3)]
            col1 = [j1t[a, c, k] for k in range(3)]
            adj = [cross(col1, col2), cross(col2, col0), cross(col0, col1)]
            s = [[s1[a, n, f] for f in range(5)], [s2[n, f] for f in range(5)], [slopes3[f][c] for f in range(5)]]
            vn = [dot3(adj[d], node.v) for d in range(3)]
            back = node.volume(adj, s, vn)
            if b == 0:
                back[1] = add3(back[1], node.face(adj[1], vn[1], [yj[0, c, f] for f in range(5)], -1))
            if b == 3:
                back[1] = add3(back[1], node.face(adj[1], vn[1], [yj[1, c, f] for f in range(5)], 1))
            if c == 0:
                back[2] = add3(back[2], node.face(adj[2], vn[2], zbot, -1))
            if c == 3:
                back[2] = add3(back[2], node.face(adj[2], vn[2], ztop, 1))
            grads = node.gradient()
            for f in range(5):
                grad_ref[f, n] = wa * grads[f]
            back0 = add3(cross(back[1], col2), cross(col1, back[2]))
            back1 = add3(cross(col2, back[0]), cross(back[2], col0))
            back2 = add3(back2, add3(cross(back[0], col1), cross(col0, back[1])))
            for k in range(3):
                j0b[b, c, k] = j0b[b, c, k] + wa * back0[k]
                j1b[a, c, k] = back1[k] if b == 0 else j1b[a, c, k] + back1[k]
        for k in range(3):
            j2b[a, b, k] = back2[k]

    @pl.when(a == 3)
    def _():
        for c in range(3):
            gx = [[[None, None], [None, None]], [[None, None], [None, None]]]
            for d in range(3):
                table = [j0b, j1b, j2b][d]
                ends = [[], []]
                for i in range(4):
                    low, high = gather_back([table[i, j, c] for j in range(4)])
                    if d:
                        low, high = WEIGHTS[i] * low, WEIGHTS[i] * high
                    ends[0].append(low)
                    ends[1].append(high)
                for j in range(2):
                    pair = gather_back(ends[j])
                    for i in range(2):
                        half = 0.5 * pair[i]
                        low = [(0, i, j), (i, 0, j), (i, j, 0)][d]
                        high = [(1, i, j), (i, 1, j), (i, j, 1)][d]
                        gx[high[0]][high[1]][high[2]] = add(gx[high[0]][high[1]][high[2]], half)
                        gx[low[0]][low[1]][low[2]] = add(gx[low[0]][low[1]][low[2]], -half)
            for e1 in range(2):
                for e2 in range(2):
                    g_ref[e1, c, e2] = gx[e1][e2][0] + pltpu.roll(gx[e1][e2][1], 1, 1)


def face_kernel(nb, cap, px, u_ref, lam_ref, disp_ref, lower_ref, upper_ref, g_ref, blk_ref, yup_ref, far_ref, rank_ref, cpack_ref, grad_in_ref, grad_ref, buf_ref, part_ref, row_ref, ubuf, lbuf, rbuf, gbuf, lhs, rhs, sem):
    index = lax.axis_index("px")
    is_first = index == 0
    is_last = index == px - 1
    copies = []
    for side in range(2):
        nodes = pl.ds(48 * side, 16)
        sources = [
            (u_ref.at[:, nodes], ubuf),
            (lam_ref.at[:, nodes], lbuf),
            (upper_ref if side else lower_ref, rbuf),
            (grad_in_ref.at[:, nodes], gbuf),
        ]
        group = [
            pltpu.make_async_copy(source, target.at[side], sem.at[side, i])
            for i, (source, target) in enumerate(sources)
        ]
        for copy in group:
            copy.start()
        copies.append(group)

    def run(side, wall, scale, sigma):
        col1 = [[None] * 3 for _ in range(4)]
        col2 = [[None] * 3 for _ in range(4)]
        for k in range(3):
            x = [[corner(disp_ref, k, side, e2, e3) for e3 in range(2)] for e2 in range(2)]
            along1 = spread(0.5 * (x[1][0] - x[0][0]), 0.5 * (x[1][1] - x[0][1]))
            along2 = spread(0.5 * (x[0][1] - x[0][0]), 0.5 * (x[1][1] - x[1][0]))
            for i in range(4):
                col1[i][k] = along1[i] + 0.5 if k == 1 else along1[i]
                col2[i][k] = along2[i] + 0.5 if k == 2 else along2[i]
        back1 = [None] * 4
        back2 = [None] * 4
        for b in range(4):
            for c in range(4):
                n = 4 * b + c
                weight = float(WEIGHTS[b] * WEIGHTS[c])
                u = [ubuf[side, f, n] for f in range(5)]
                own = [lbuf[side, f, n] for f in range(5)]
                normal = cross(col1[c], col2[b])
                if wall:
                    inverse, v, v2, p, ep = primitives(u)
                    vn = dot3(normal, v)
                    m = u[1:4]
                    jump = [-weight * own[f] for f in range(1, 4)]
                    square = dot3(normal, normal)
                    root = lax.rsqrt(square)
                    rate = vn * (root * root)
                    q = u[0] * vn
                    level = dot3(jump, normal)
                    slope = 2.0 * (rate - root)
                    phi = q * (rate - 2.0 * root) + p
                    lk = level * slope
                    along = lk * q * (root * root)
                    grads = [level * (0.2 * v2 - rate * vn)]
                    for k in range(3):
                        grads.append(lk * normal[k] - (0.4 * level) * v[k])
                    grads.append(0.4 * level)
                    back = [jump[k] * phi + lk * m[k] - along * normal[k] for k in range(3)]
                else:
                    node = Node(u)
                    vn = dot3(normal, node.v)
                    factor = scale * weight
                    jump = [factor * (own[f] - rbuf[side, f, n]) for f in range(5)]
                    back = node.face(normal, vn, jump, sigma)
                    grads = node.gradient()
                for f in range(5):
                    gbuf[side, f, n] = gbuf[side, f, n] + grads[f]
                back1[c] = add3(back1[c], cross(col2[b], back))
                back2[b] = add3(back2[b], cross(back, col1[c]))
        rows = lax.broadcasted_iota(jnp.int32, (8, 128), 0)
        for k in range(3):
            low1, high1 = gather_back([back1[i][k] for i in range(4)])
            low2, high2 = gather_back([back2[i][k] for i in range(4)])
            gx = [[-0.5 * (low1 + low2), 0.5 * (low2 - high1)], [0.5 * (low1 - high2), 0.5 * (high1 + high2)]]
            near = g_ref[side, k, 0] + gx[0][0] + pltpu.roll(gx[0][1], 1, 1)
            far = g_ref[side, k, 1] + gx[1][0] + pltpu.roll(gx[1][1], 1, 1)
            part_ref[side, k] = near + jnp.where(rows == 0, 0.0, pltpu.roll(far, 1, 0))
            row_ref[3 * side + k : 3 * side + k + 1, :] = far[7:8, :]

    for copy in copies[0]:
        copy.wait()

    @pl.when(is_first)
    def _():
        run(0, True, None, None)

    @pl.when(jnp.logical_not(is_first))
    def _():
        run(0, False, -0.5, -1)

    back0 = pltpu.make_async_copy(gbuf.at[0], grad_ref.at[:, pl.ds(0, 16)], sem.at[0, 4])
    back0.start()
    for copy in copies[1]:
        copy.wait()
    run(1, False, jnp.where(is_last, F32(1.0), F32(0.5)), jnp.where(is_last, F32(0.0), F32(1.0)))
    back1 = pltpu.make_async_copy(gbuf.at[1], grad_ref.at[:, pl.ds(48, 16)], sem.at[1, 4])
    back1.start()

    block_of = lax.broadcasted_iota(jnp.int32, (nb, 128), 0).astype(F32)
    slot_of = (lax.broadcasted_iota(jnp.int32, (128, 128), 0) & (cap - 1)).astype(F32)
    sums = []
    for stream, count in enumerate((8, 8, 1, 1)):
        for y in range(count):
            block, values, ranks = [
                (blk_ref[y : y + 1, :], lambda k: part_ref[0, k, y : y + 1, :], y),
                (far_ref[y : y + 1, :], lambda k: part_ref[1, k, y : y + 1, :], 8 + y),
                (yup_ref[80:81, :], lambda k: row_ref[k : k + 1, :], 16),
                (far_ref[8:9, :], lambda k: row_ref[3 + k : 4 + k, :], 17),
            ][stream]
            lanes = pl.ds(128 * y, 128)
            here = jnp.broadcast_to(block, (nb, 128)) == block_of
            rhs[:, lanes] = jnp.where(
                jnp.broadcast_to(rank_ref[ranks : ranks + 1, :], (128, 128)) == slot_of, 1.0, 0.0
            ).astype(jnp.bfloat16)
            for k in range(3):
                row = values(k)
                high = row.astype(jnp.bfloat16).astype(F32)
                for part, piece in enumerate((high, row - high)):
                    lhs[pl.ds((3 * part + k) * nb, nb), lanes] = jnp.where(
                        here, jnp.broadcast_to(piece, (nb, 128)), 0.0
                    ).astype(jnp.bfloat16)
        total = lax.dot_general(
            lhs[:, pl.ds(0, 128 * count)],
            rhs[:, pl.ds(0, 128 * count)],
            (((1,), (1,)), ((), ())),
            preferred_element_type=F32,
        )
        total = total[0 : 3 * nb] + total[3 * nb : 6 * nb]
        sums.append([total[k * nb : (k + 1) * nb] for k in range(3)])
    items = [sums[stream][k] for k in range(3) for stream in range(4)]
    items += [cpack_ref[pl.ds(k * nb, nb), :] for k in range(3)]
    per_row = 128 // cap
    height = buf_ref.shape[0] // nb
    position = lax.broadcasted_iota(jnp.int32, (nb, 128), 1) // cap
    for r in range(height):
        inside = items[r * per_row : (r + 1) * per_row]
        value = inside[0]
        for i, item in enumerate(inside[1:], 1):
            value = jnp.where(position == i, item, value)
        buf_ref[pl.ds(r, nb, stride=height), :] = value
    back0.wait()
    back1.wait()


def slot_kernel(nb, cap, blk_ref, yup_ref, far_ref, coords_ref, rank_ref, cpack_ref, lhs, rhs):
    block_of = lax.broadcasted_iota(jnp.int32, (nb, 128), 0).astype(F32)
    k_of = lax.broadcasted_iota(jnp.int32, (128, 256), 0)
    z_of = lax.broadcasted_iota(jnp.int32, (128, 256), 1)
    before = jnp.where((k_of < z_of) | (z_of >= 128), 1.0, 0.0).astype(jnp.bfloat16)
    slot_of = (lax.broadcasted_iota(jnp.int32, (128, 128), 0) & (cap - 1)).astype(F32)
    for stream, count in enumerate((8, 8, 1, 1)):
        offset = jnp.zeros((nb, 128), F32)
        for y in range(count):
            block, slot = [
                (blk_ref[y : y + 1, :], y),
                (far_ref[y : y + 1, :], 8 + y),
                (yup_ref[80:81, :], 16),
                (far_ref[8:9, :], 17),
            ][stream]
            here = jnp.where(jnp.broadcast_to(block, (nb, 128)) == block_of, 1.0, 0.0)
            counts = jnp.dot(here.astype(jnp.bfloat16), before, preferred_element_type=F32)
            rank = jnp.sum(here * (counts[:, 0:128] + offset), axis=0, keepdims=True)
            offset = offset + counts[:, 128:256]
            rank_ref[slot : slot + 1, :] = rank
            if stream == 0:
                lanes = pl.ds(128 * y, 128)
                rhs[:, lanes] = jnp.where(
                    jnp.broadcast_to(rank, (128, 128)) == slot_of, 1.0, 0.0
                ).astype(jnp.bfloat16)
                for k in range(3):
                    rest = coords_ref[k : k + 1, lanes]
                    for part in range(3):
                        piece = rest.astype(jnp.bfloat16).astype(F32)
                        rest = rest - piece
                        lhs[pl.ds((3 * part + k) * nb, nb), lanes] = (
                            here * jnp.broadcast_to(piece, (nb, 128))
                        ).astype(jnp.bfloat16)
        if stream == 0:
            total = lax.dot_general(
                lhs[...], rhs[...], (((1,), (1,)), ((), ())), preferred_element_type=F32
            )
            cpack_ref[...] = total[0 : 3 * nb] + total[3 * nb : 6 * nb] + total[6 * nb : 9 * nb]


def powers(t, degree):
    out = [None, t]
    for n in range(2, degree + 1):
        out.append(out[n // 2] * out[n - n // 2])
    return out


def bernstein(t, degree):
    up = powers(t, degree)
    down = powers(1.0 - t, degree)
    out = []
    for a in range(degree + 1):
        if a == 0:
            out.append(down[degree])
        elif a == degree:
            out.append(up[degree])
        else:
            out.append(float(math.comb(degree, a)) * up[a] * down[degree - a])
    return out


def lattice_kernel(nb, cap, py, buf_ref, part_ref, yrow_ref, xrow_ref, owned_ref, out_ref, lhs, rhs):
    rows = lax.broadcasted_iota(jnp.int32, (8, 128), 0)
    for k in range(3):
        beside = jnp.broadcast_to(yrow_ref[k : k + 1, :], (8, 128))
        owned_ref[k] = part_ref[0, k] + jnp.where(rows == 0, beside, 0.0) + xrow_ref[k]

    per_row = 128 // cap
    height = buf_ref.shape[0] // nb
    source = lax.broadcasted_iota(jnp.int32, (nb, 128), 0)
    lane = lax.broadcasted_iota(jnp.int32, (16, 128), 1)

    def item(j):
        value = buf_ref[pl.ds(j // per_row, nb, stride=height), :]
        at = j % per_row
        return pltpu.roll(value, 128 - at * cap, 1) if at else value

    def from_px(value):
        return jnp.where(source >= py, pltpu.roll(value, py, 0), 0.0)

    def from_py(value):
        return jnp.where(source % py > 0, pltpu.roll(value, 1, 0), pltpu.roll(value, nb - (py - 1), 0))

    def dense(value):
        out = value[0:16]
        for i in range(1, per_row):
            piece = pltpu.roll(value[16 * i : 16 * (i + 1)], i * cap, 1)
            out = jnp.where(lane // cap == i, piece, out)
        return out

    sens = []
    for k in range(3):
        own, above, beside, across = [item(4 * k + stream) for stream in range(4)]
        sens.append(dense(own + from_py(beside) + from_px(above + from_py(across))))
    u, v, w = [dense(item(12 + k)) for k in range(3)]
    bu = bernstein(u, LU - 1)
    bv = bernstein(v, LV - 1)
    bw = bernstein(w, LW - 1)
    for a in range(LU):
        for k in range(3):
            lhs[pl.ds(16 * (3 * a + k), 16), :] = sens[k] * bu[a]
    for b in range(LV):
        for c in range(LW):
            rhs[pl.ds(16 * (LW * b + c), 16), :] = bv[b] * bw[c]
    left = jnp.concatenate([lhs[pl.ds(i, 3 * LU, stride=16), :] for i in range(16)], axis=1)
    right = jnp.concatenate([rhs[pl.ds(i, LV * LW, stride=16), :] for i in range(16)], axis=1)
    left_high = left.astype(jnp.bfloat16)
    left_low = (left - left_high.astype(F32)).astype(jnp.bfloat16)
    right_high = right.astype(jnp.bfloat16)
    right_low = (right - right_high.astype(F32)).astype(jnp.bfloat16)

    def product(x, y):
        return lax.dot_general(x, y, (((1,), (1,)), ((), ())), preferred_element_type=F32)

    total = product(left_high, right_high) + (product(left_high, right_low) + product(left_low, right_high))
    for a in range(LU):
        out_ref[:, pl.ds(LV * LW * a, LV * LW)] = total[3 * a : 3 * a + 3, :]


def volume_call(u, lam, disp, yup, ydn):
    tile = (8, 128)
    whole = lambda shape: pl.BlockSpec(shape, lambda a: (0,) * len(shape))
    return pl.pallas_call(
        volume_kernel,
        grid=(4,),
        in_specs=[
            pl.BlockSpec((5, 16) + tile, lambda a: (0, a, 0, 0)),
            whole(lam.shape),
            whole(disp.shape),
            whole(yup.shape),
            whole(ydn.shape),
        ],
        out_specs=[
            pl.BlockSpec((5, 16) + tile, lambda a: (0, a, 0, 0)),
            whole((2, 3, 2) + tile),
        ],
        out_shape=[
            jax.ShapeDtypeStruct((5, 64) + tile, F32),
            jax.ShapeDtypeStruct((2, 3, 2) + tile, F32),
        ],
        scratch_shapes=[pltpu.VMEM((4, 4, 3) + tile, F32)] * 6
        + [
            pltpu.VMEM((4, 16, 5) + tile, F32),
            pltpu.VMEM((16, 5) + tile, F32),
            pltpu.VMEM((2, 4, 5) + tile, F32),
        ],
        name="volume",
    )(u, lam, disp, yup, ydn)


def face_call(u, lam, disp, lower, upper, g, blk, yup, far, ranks, cpack, grad, nb, cap, px):
    tile = (8, 128)
    vmem = pl.BlockSpec(memory_space=pltpu.VMEM)
    hbm = pl.BlockSpec(memory_space=pl.ANY)
    height = -(-15 * cap // 128)
    return pl.pallas_call(
        functools.partial(face_kernel, nb, cap, px),
        in_specs=[hbm, hbm, vmem, hbm, hbm, vmem, vmem, vmem, vmem, vmem, vmem, hbm],
        out_specs=[hbm, vmem, vmem, vmem],
        out_shape=[
            jax.ShapeDtypeStruct((5, 64) + tile, F32),
            jax.ShapeDtypeStruct((nb * height, 128), F32),
            jax.ShapeDtypeStruct((2, 3) + tile, F32),
            jax.ShapeDtypeStruct((6, 128), F32),
        ],
        scratch_shapes=[pltpu.VMEM((2, 5, 16) + tile, F32)] * 4
        + [
            pltpu.VMEM((6 * nb, 1024), jnp.bfloat16),
            pltpu.VMEM((128, 1024), jnp.bfloat16),
            pltpu.SemaphoreType.DMA((2, 5)),
        ],
        input_output_aliases={11: 0},
        name="faces",
    )(u, lam, disp, lower, upper, g, blk, yup, far, ranks, cpack, grad)


def slot_call(blk, yup, far, coords, nb, cap):
    return pl.pallas_call(
        functools.partial(slot_kernel, nb, cap),
        out_shape=[
            jax.ShapeDtypeStruct((24, 128), F32),
            jax.ShapeDtypeStruct((3 * nb, 128), F32),
        ],
        scratch_shapes=[
            pltpu.VMEM((9 * nb, 1024), jnp.bfloat16),
            pltpu.VMEM((128, 1024), jnp.bfloat16),
        ],
        name="slots",
    )(blk, yup, far, coords)


def lattice_call(buf, part, yrow, xrow, nb, cap, py):
    return pl.pallas_call(
        functools.partial(lattice_kernel, nb, cap, py),
        out_shape=[
            jax.ShapeDtypeStruct((3, 8, 128), F32),
            jax.ShapeDtypeStruct((3, LU * LV * LW), F32),
        ],
        scratch_shapes=[
            pltpu.VMEM((16 * 3 * LU, 128), F32),
            pltpu.VMEM((16 * LV * LW, 128), F32),
        ],
        name="lattice",
    )(buf, part, yrow, xrow)


def shift_px(payload, step):
    length = lax.axis_size("px")
    pairs = [(i, i + step) for i in range(length) if 0 <= i + step < length]
    return lax.ppermute(payload, "px", pairs)


def shift_py(payload, step):
    length = lax.axis_size("py")
    return lax.ppermute(payload, "py", [(i, (i + step) % length) for i in range(length)])


def per_device(flow_state, adjoint, displacement, lattice_block, lattice_coords):
    px = lax.axis_size("px")
    py = lax.axis_size("py")
    nb = px * py
    cap = 2 * 1024 // nb
    u = flow_state.reshape(5, 64, 8, 128)
    lam = adjoint.reshape(5, 64, 8, 128)
    blk = lattice_block.reshape(8, 128).astype(F32)
    coords = lattice_coords.reshape(3, 1024)
    upper = shift_px(lam[:, 0:16], -1)
    lower = shift_px(lam[:, 48:64], 1)
    cube = lam.reshape(5, 4, 4, 4, 8, 128)
    yup = shift_py(jnp.concatenate([cube[:, :, 0, :, 0, :].reshape(80, 128), blk[0:1]]), -1)
    ydn = shift_py(cube[:, :, 3, :, 7, :].reshape(80, 128), 1)
    far = shift_px(jnp.concatenate([blk, yup[80:81]]), -1)
    grad, g = volume_call(u, lam, displacement, yup, ydn)
    ranks, cpack = slot_call(blk, yup, far, coords, nb, cap)
    grad, buf, part, rows = face_call(
        u, lam, displacement, lower, upper, g, blk, yup, far, ranks, cpack, grad, nb, cap, px
    )
    received = lax.all_to_all(buf, ("px", "py"), split_axis=0, concat_axis=0, tiled=True)
    yrow = shift_py(rows, 1)
    xrow = shift_px(part[1].at[:, 0, :].add(yrow[3:6]), 1)
    owned, lattice = lattice_call(received, part, yrow, xrow, nb, cap, py)
    return (
        grad.reshape(5, 64, 1, 8, 128),
        owned.reshape(3, 1, 8, 128),
        lattice.reshape(1, 1, 3, LU * LV * LW),
    )


def solution(mesh):
    in_specs = (
        P(None, None, "px", "py", None),
        P(None, None, "px", "py", None),
        P(None, "px", "py", None),
        P("px", "py", None, None),
        P("px", "py", None, None),
    )
    out_specs = (
        P(None, None, "px", "py", None),
        P(None, "px", "py", None),
        P("px", "py", None, None),
    )
    return jax.shard_map(
        per_device, mesh=mesh, in_specs=in_specs, out_specs=out_specs, check_vma=False
    )
```

```python
import functools
import math

import jax
import jax.numpy as jnp
import numpy as np
from jax import lax
from jax.experimental import pallas as pl
from jax.experimental.pallas import tpu as pltpu
from jax.sharding import PartitionSpec as P

LU = 12
LV = 12
LW = 6
F32 = jnp.float32
POINTS = [-1.0, -1.0 / math.sqrt(5.0), 1.0 / math.sqrt(5.0), 1.0]
WEIGHTS = [1.0 / 6.0, 5.0 / 6.0, 5.0 / 6.0, 1.0 / 6.0]
UPPER = [0.5 * (1.0 + point) for point in POINTS]


def derivative_matrix():
    matrix = np.zeros((4, 4))
    for target in range(4):
        for source in range(4):
            others = [m for m in range(4) if m != source]
            if target == source:
                matrix[target, source] = sum(1.0 / (POINTS[source] - POINTS[m]) for m in others)
            else:
                upper = np.prod([POINTS[target] - POINTS[m] for m in others if m != target])
                lower = np.prod([POINTS[source] - POINTS[m] for m in others])
                matrix[target, source] = upper / lower
    return matrix


DM = derivative_matrix()


def line_slopes(line, scale):
    e0 = line[0] + line[3]
    o0 = line[0] - line[3]
    e1 = line[1] + line[2]
    o1 = line[1] - line[2]
    even = e0 - e1
    out = [None] * 4
    for m in range(2):
        half = 0.5 * scale[m]
        p0 = float(half * (DM[m, 0] - DM[m, 3]))
        p1 = float(half * (DM[m, 1] - DM[m, 2]))
        k = float(half * (DM[m, 0] + DM[m, 3]))
        odd_part = p0 * o0 + p1 * o1
        even_part = k * even
        out[m] = odd_part + even_part
        out[3 - m] = odd_part - even_part
    return out


def spread(low, high):
    step = high - low
    return [low, low + float(UPPER[1]) * step, low + float(UPPER[2]) * step, high]


def gather_back(g):
    middle = float(UPPER[1]) * g[1] + float(UPPER[2]) * g[2]
    return (g[0] + g[1] + g[2] - middle, g[3] + middle)


def cross(x, y):
    return [x[1] * y[2] - x[2] * y[1], x[2] * y[0] - x[0] * y[2], x[0] * y[1] - x[1] * y[0]]


def dot3(x, y):
    return x[0] * y[0] + x[1] * y[1] + x[2] * y[2]


def add(x, y):
    return y if x is None else x + y


def add3(x, y):
    return y if x is None else [x[i] + y[i] for i in range(3)]


def primitives(u):
    inverse = 1.0 / u[0]
    v = [u[1] * inverse, u[2] * inverse, u[3] * inverse]
    mv = u[1] * v[0] + u[2] * v[1] + u[3] * v[2]
    p = 0.4 * u[4] - 0.2 * mv
    return inverse, v, mv * inverse, p, u[4] + p


class Node:
    def __init__(self, u):
        self.inverse, self.v, self.v2, self.p, self.ep = primitives(u)
        self.big = [u[0], u[1], u[2], u[3], self.ep]
        self.w = [None] * 5
        self.pb = None
        self.b = None

    def work(self, s):
        return sum((s[f] * self.big[f] for f in range(1, 5)), s[0] * self.big[0])

    def volume(self, adj, s, vn):
        back = []
        for d in range(3):
            k = self.work(s[d])
            for f in range(5):
                self.w[f] = add(self.w[f], vn[d] * s[d][f])
            self.pb = add(self.pb, dot3(adj[d], s[d][1:4]))
            self.b = add3(self.b, [adj[d][c] * k for c in range(3)])
            back.append([self.v[c] * k + self.p * s[d][1 + c] for c in range(3)])
        self.pb = self.pb + self.w[4]
        return back

    def face(self, n, vn, jump, sigma):
        k = self.work(jump)
        square = dot3(n, n)
        root = lax.rsqrt(square)
        twice = 2.0 * root
        length = twice * square
        if isinstance(sigma, int) and sigma == 1:
            cf = vn + length
        elif isinstance(sigma, int):
            cf = vn - length
            twice = -twice
        else:
            cf = vn + sigma * length
            twice = sigma * twice
        q = k - jump[4] * self.p
        along = twice * q
        for f in range(5):
            self.w[f] = add(self.w[f], cf * jump[f])
        self.pb = add(self.pb, dot3(n, jump[1:4]) + vn * jump[4])
        self.b = add3(self.b, [n[c] * k for c in range(3)])
        return [self.v[c] * k + self.p * jump[1 + c] + n[c] * along for c in range(3)]

    def gradient(self):
        pb4 = 0.4 * self.pb
        rb = [self.b[c] * self.inverse for c in range(3)]
        out = [self.w[0] - dot3(self.v, rb) + (0.5 * pb4) * self.v2]
        for c in range(3):
            out.append(self.w[1 + c] + rb[c] - pb4 * self.v[c])
        out.append(self.w[4] + pb4)
        return out


def corner(disp_ref, c, e1, e2):
    return disp_ref[pl.ds(9 * c + e2, 8), e1, :]


def with_next(window):
    return [window, pltpu.roll(window, 127, 1)]


def trace_kernel(lam_ref, cube_ref, blk_ref, coords_ref, disp_ref, own_even, own_odd, y_even, y_odd, blkf, coords, disp, tiles, blocks, sem):
    x_odd = lax.axis_index("px") % 2
    y_up = 1 - lax.axis_index("py") % 2
    copies = [
        pltpu.make_async_copy(lam_ref.at[:, pl.ds(48 - 48 * x_odd, 16)], own_even, sem.at[0]),
        pltpu.make_async_copy(lam_ref.at[:, pl.ds(48 * x_odd, 16)], own_odd, sem.at[1]),
        pltpu.make_async_copy(cube_ref.at[:, :, 0], tiles.at[0], sem.at[2]),
        pltpu.make_async_copy(cube_ref.at[:, :, 3], tiles.at[1], sem.at[3]),
        pltpu.make_async_copy(blk_ref, blocks, sem.at[4]),
        pltpu.make_async_copy(coords_ref, coords, sem.at[5]),
        pltpu.make_async_copy(disp_ref, disp, sem.at[6]),
    ]
    for copy in copies:
        copy.start()
    for copy in copies[2:5]:
        copy.wait()
    blkf[...] = blocks[...].astype(F32)
    rows = tiles.reshape(1280, 128)
    bottom = rows[pl.ds(0, 80, stride=8), :]
    top = rows[pl.ds(640 + 7, 80, stride=8), :]
    y_even[0:80, :] = jnp.where(y_up == 1, top, bottom)
    y_odd[0:80, :] = jnp.where(y_up == 1, bottom, top)
    first_row = blocks[0:1, :].astype(F32)
    y_even[80:81, :] = first_row
    y_odd[80:81, :] = first_row
    for copy in copies[:2] + copies[5:]:
        copy.wait()


def volume_kernel(u_ref, lam_ref, disp_ref, even_ref, odd_ref, grad_ref, ukeep, gkeep, cols, g_ref, lam, umid, gmid, j0t, j1t, j2t, j0b, j1b, j2b, s1, s2, yj, sem):
    lam_copies = [pltpu.make_async_copy(lam_ref.at[f], lam.at[f], sem.at[f]) for f in range(5)]
    u_at = [ukeep.at[0], umid.at[0], umid.at[1], ukeep.at[1]]
    g_at = [gkeep.at[0], gmid.at[0], gmid.at[1], gkeep.at[1]]
    u_copies = [pltpu.make_async_copy(u_ref.at[:, pl.ds(16 * a, 16)], u_at[a], sem.at[5 + a]) for a in range(4)]
    for copy in lam_copies + u_copies:
        copy.start()

    for c in range(3):
        x = [[with_next(corner(disp_ref, c, e1, e2)) for e2 in range(2)] for e1 in range(2)]
        for d in range(3):
            ends = []
            for i in range(2):
                pair = []
                for j in range(2):
                    low = [(0, i, j), (i, 0, j), (i, j, 0)][d]
                    high = [(1, i, j), (i, 1, j), (i, j, 1)][d]
                    half = 0.5 * (x[high[0]][high[1]][high[2]] - x[low[0]][low[1]][low[2]])
                    pair.append(half + 0.5 if c == d else half)
                ends.append(spread(pair[0], pair[1]))
            for j in range(4):
                values = spread(ends[0][j], ends[1][j])
                for i in range(4):
                    [j0t, j1t, j2t][d][i, j, c] = values[i]
                    if d and i in (0, 3):
                        cols[i // 3, d - 1, j, c] = values[i]
    for f in range(5):
        lam_copies[f].wait()
        for b in range(4):
            for c in range(4):
                line = [lam[f, 16 * i + 4 * b + c] for i in range(4)]
                out = line_slopes(line, [-WEIGHTS[i] * WEIGHTS[b] * WEIGHTS[c] for i in range(4)])
                for i in range(4):
                    s1[i, 4 * b + c, f] = out[i]

    above_even = lax.axis_index("py") % 2 == 0
    rows = lax.broadcasted_iota(jnp.int32, (8, 128), 0)
    first_row = rows == 0
    last_row = rows == 7
    mid_copies = []
    for a in range(4):
        base = 16 * a
        wa = WEIGHTS[a]
        u_copies[a].wait()
        for f in range(5):
            for c in range(4):
                line = [lam[f, base + 4 * b + c] for b in range(4)]
                out = line_slopes(line, [-wa * WEIGHTS[b] * WEIGHTS[c] for b in range(4)])
                for b in range(4):
                    s2[4 * b + c, f] = out[b]
                half = float(0.5 * wa * WEIGHTS[c])
                at = f * 16 + a * 4 + c
                one = jnp.broadcast_to(even_ref[at : at + 1, :], TILE)
                two = jnp.broadcast_to(odd_ref[at : at + 1, :], TILE)
                above = jnp.where(above_even, one, two)
                below = jnp.where(above_even, two, one)
                plus = jnp.where(last_row, above, pltpu.roll(line[0], 7, 0))
                top = half * (line[3] - plus)
                bottom = half * (below - line[0])
                yj[1, c, f] = top
                yj[0, c, f] = jnp.where(first_row, bottom, pltpu.roll(top, 1, 0))
        for b in range(4):
            slopes3 = []
            ztop = []
            zbot = []
            half = float(0.5 * wa * WEIGHTS[b])
            for f in range(5):
                line = [lam[f, base + 4 * b + c] for c in range(4)]
                slopes3.append(line_slopes(line, [-wa * WEIGHTS[b] * WEIGHTS[c] for c in range(4)]))
                top = half * (line[3] - pltpu.roll(line[0], 127, 1))
                ztop.append(top)
                zbot.append(pltpu.roll(top, 1, 1))
            back2 = None
            col2 = [j2t[a, b, k] for k in range(3)]
            for c in range(4):
                n = 4 * b + c
                node = Node([u_at[a][f, n] for f in range(5)])
                col0 = [j0t[b, c, k] for k in range(3)]
                col1 = [j1t[a, c, k] for k in range(3)]
                adj = [cross(col1, col2), cross(col2, col0), cross(col0, col1)]
                s = [[s1[a, n, f] for f in range(5)], [s2[n, f] for f in range(5)], [slopes3[f][c] for f in range(5)]]
                vn = [dot3(adj[d], node.v) for d in range(3)]
                back = node.volume(adj, s, vn)
                if b == 0:
                    back[1] = add3(back[1], node.face(adj[1], vn[1], [yj[0, c, f] for f in range(5)], -1))
                if b == 3:
                    back[1] = add3(back[1], node.face(adj[1], vn[1], [yj[1, c, f] for f in range(5)], 1))
                if c == 0:
                    back[2] = add3(back[2], node.face(adj[2], vn[2], zbot, -1))
                if c == 3:
                    back[2] = add3(back[2], node.face(adj[2], vn[2], ztop, 1))
                grads = node.gradient()
                for f in range(5):
                    g_at[a][f, n] = grads[f]
                back0 = add3(cross(back[1], col2), cross(col1, back[2]))
                back1 = add3(cross(col2, back[0]), cross(back[2], col0))
                back2 = add3(back2, add3(cross(back[0], col1), cross(col0, back[1])))
                for k in range(3):
                    j0b[b, c, k] = back0[k] if a == 0 else j0b[b, c, k] + back0[k]
                    j1b[a, c, k] = back1[k] if b == 0 else j1b[a, c, k] + back1[k]
            for k in range(3):
                j2b[a, b, k] = back2[k]
        if a in (1, 2):
            copy = pltpu.make_async_copy(gmid.at[a - 1], grad_ref.at[:, pl.ds(base, 16)], sem.at[8 + a])
            copy.start()
            mid_copies.append(copy)

    for c in range(3):
        gx = [[[None, None], [None, None]], [[None, None], [None, None]]]
        for d in range(3):
            table = [j0b, j1b, j2b][d]
            ends = [[], []]
            for i in range(4):
                low, high = gather_back([table[i, j, c] for j in range(4)])
                ends[0].append(low)
                ends[1].append(high)
            for j in range(2):
                pair = gather_back(ends[j])
                for i in range(2):
                    half = 0.5 * pair[i]
                    low = [(0, i, j), (i, 0, j), (i, j, 0)][d]
                    high = [(1, i, j), (i, 1, j), (i, j, 1)][d]
                    gx[high[0]][high[1]][high[2]] = add(gx[high[0]][high[1]][high[2]], half)
                    gx[low[0]][low[1]][low[2]] = add(gx[low[0]][low[1]][low[2]], -half)
        for e1 in range(2):
            for e2 in range(2):
                g_ref[e1, c, e2] = gx[e1][e2][0] + pltpu.roll(gx[e1][e2][1], 1, 1)
    for copy in mid_copies:
        copy.wait()


def one_side(side, scale, sigma, wall, u_ref, own_ref, received_ref, gkeep, cols, g_ref, grad_ref, part_ref, row_ref, gout, sem):
    col1 = [[cols[side, 0, c, k] for k in range(3)] for c in range(4)]
    back1 = [None] * 4
    back2 = [None] * 4
    for b in range(4):
        col2 = [cols[side, 1, b, k] for k in range(3)]
        for c in range(4):
            n = 4 * b + c
            weight = float(WEIGHTS[b] * WEIGHTS[c])
            u = [u_ref[side, f, n] for f in range(5)]
            own = [own_ref[f, n] for f in range(5)]
            normal = cross(col1[c], col2)
            if wall:
                inverse, v, v2, p, ep = primitives(u)
                vn = dot3(normal, v)
                m = u[1:4]
                jump = [-weight * own[f] for f in range(1, 4)]
                square = dot3(normal, normal)
                root = lax.rsqrt(square)
                rate = vn * (root * root)
                q = u[0] * vn
                level = dot3(jump, normal)
                slope = 2.0 * (rate - root)
                phi = q * (rate - 2.0 * root) + p
                lk = level * slope
                along = lk * q * (root * root)
                grads = [level * (0.2 * v2 - rate * vn)]
                for k in range(3):
                    grads.append(lk * normal[k] - (0.4 * level) * v[k])
                grads.append(0.4 * level)
                back = [jump[k] * phi + lk * m[k] - along * normal[k] for k in range(3)]
            else:
                node = Node(u)
                vn = dot3(normal, node.v)
                factor = scale * weight
                jump = [factor * (own[f] - received_ref[f, n]) for f in range(5)]
                back = node.face(normal, vn, jump, sigma)
                grads = node.gradient()
            for f in range(5):
                gout[f, n] = gkeep[side, f, n] + grads[f]
            back1[c] = add3(back1[c], cross(col2, back))
            back2[b] = add3(back2[b], cross(back, col1[c]))
        pltpu.make_async_copy(
            gout.at[:, pl.ds(4 * b, 4)], grad_ref.at[:, pl.ds(48 * side + 4 * b, 4)], sem.at[b]
        ).start()
    rows = lax.broadcasted_iota(jnp.int32, TILE, 0)
    for k in range(3):
        low1, high1 = gather_back([back1[i][k] for i in range(4)])
        low2, high2 = gather_back([back2[i][k] for i in range(4)])
        gx = [[-0.5 * (low1 + low2), 0.5 * (low2 - high1)], [0.5 * (low1 - high2), 0.5 * (high1 + high2)]]
        near = g_ref[side, k, 0] + gx[0][0] + pltpu.roll(gx[0][1], 1, 1)
        far = g_ref[side, k, 1] + gx[1][0] + pltpu.roll(gx[1][1], 1, 1)
        part_ref[side, k] = near + jnp.where(rows == 0, 0.0, pltpu.roll(far, 1, 0))
        row_ref[pl.ds(3 * side + k, 1), :] = far[7:8, :]


def wait_side(side, grad_ref, gout, sem):
    for b in range(4):
        pltpu.make_async_copy(
            gout.at[:, pl.ds(4 * b, 4)], grad_ref.at[:, pl.ds(48 * side + 4 * b, 4)], sem.at[b]
        ).wait()


def block_ranks(nb, groups, emit):
    block_of = lax.broadcasted_iota(jnp.int32, (nb, 128), 0).astype(F32)
    k_of = lax.broadcasted_iota(jnp.int32, (128, 256), 0)
    z_of = lax.broadcasted_iota(jnp.int32, (128, 256), 1)
    before = jnp.where((k_of < z_of) | (z_of >= 128), 1.0, 0.0).astype(jnp.bfloat16)
    here = [jnp.where(jnp.broadcast_to(row, (nb, 128)) == block_of, 1.0, 0.0) for row in sum(groups, [])]
    counts = jnp.dot(
        jnp.concatenate(here, axis=0).astype(jnp.bfloat16), before, preferred_element_type=F32
    )
    i = 0
    for group in groups:
        offset = None
        for _ in group:
            mine = counts[nb * i : nb * (i + 1)]
            earlier = mine[:, 0:128] if offset is None else mine[:, 0:128] + offset
            emit(i, here[i], jnp.sum(here[i] * earlier, axis=0, keepdims=True))
            offset = add(offset, mine[:, 128:256])
            i += 1


def first_face_kernel(grad_in_ref, u_ref, own_ref, received_ref, gkeep, cols, g_ref, grad_ref, part_ref, row_ref, gout, sem):
    side = 1 - lax.axis_index("px") % 2
    sign = jnp.where(side == 0, F32(-1.0), F32(1.0))
    one_side(side, 0.5 * sign, sign, False, u_ref, own_ref, received_ref, gkeep, cols, g_ref, grad_ref, part_ref, row_ref, gout, sem)
    wait_side(side, grad_ref, gout, sem)


def label_kernel(nb, even_ref, odd_ref, far_ref, row_ref, label_ref):
    beside = jnp.where(lax.axis_index("py") % 2 == 0, even_ref[80:81, :], odd_ref[80:81, :])
    across = far_ref[8:9, :]
    label_ref[0:8, :] = far_ref[0:8, :]
    label_ref[8:9, :] = beside
    label_ref[9:10, :] = across

    def emit(i, here, rank):
        label_ref[16 + i : 17 + i, :] = rank

    block_ranks(nb, [[far_ref[y : y + 1, :] for y in range(8)], [beside], [across]], emit)


def second_face_kernel(nb, cap, px, grad_in_ref, u_ref, own_ref, received_ref, gkeep, cols, g_ref, part_in_ref, row_in_ref, mine_ref, label_ref, cpack_ref, grad_ref, buf_ref, part_ref, row_ref, gout, lhs, rhs, sem):
    index = lax.axis_index("px")
    side = index % 2
    is_first = index == 0
    is_last = index == px - 1
    part_ref[1 - side] = part_in_ref[1 - side]
    row_ref[...] = row_in_ref[...]
    rest = (u_ref, own_ref, received_ref, gkeep, cols, g_ref, grad_ref, part_ref, row_ref, gout, sem)

    @pl.when(is_first)
    def _():
        one_side(side, None, None, True, *rest)

    @pl.when(jnp.logical_not(is_first))
    def _():
        scale = jnp.where(side == 0, F32(-0.5), jnp.where(is_last, F32(1.0), F32(0.5)))
        sigma = jnp.where(side == 0, F32(-1.0), jnp.where(is_last, F32(0.0), F32(1.0)))
        one_side(side, scale, sigma, False, *rest)

    block_of = lax.broadcasted_iota(jnp.int32, (nb, 128), 0).astype(F32)
    slot_of = (lax.broadcasted_iota(jnp.int32, (128, 128), 0) & (cap - 1)).astype(F32)
    sums = []
    for stream, count in enumerate((8, 8, 1, 1)):
        for y in range(count):
            block, values, rank = [
                (mine_ref[y : y + 1, :], lambda k: part_ref[0, k, y : y + 1, :], mine_ref[8 + y : 9 + y, :]),
                (label_ref[y : y + 1, :], lambda k: part_ref[1, k, y : y + 1, :], label_ref[16 + y : 17 + y, :]),
                (label_ref[8:9, :], lambda k: row_ref[k : k + 1, :], label_ref[24:25, :]),
                (label_ref[9:10, :], lambda k: row_ref[3 + k : 4 + k, :], label_ref[25:26, :]),
            ][stream]
            lanes = pl.ds(128 * y, 128)
            here = jnp.broadcast_to(block, (nb, 128)) == block_of
            rhs[:, lanes] = jnp.where(jnp.broadcast_to(rank, (128, 128)) == slot_of, 1.0, 0.0).astype(jnp.bfloat16)
            for k in range(3):
                row = values(k)
                high = row.astype(jnp.bfloat16).astype(F32)
                for part, piece in enumerate((high, row - high)):
                    lhs[pl.ds((3 * part + k) * nb, nb), lanes] = jnp.where(
                        here, jnp.broadcast_to(piece, (nb, 128)), 0.0
                    ).astype(jnp.bfloat16)
        total = lax.dot_general(
            lhs[:, pl.ds(0, 128 * count)],
            rhs[:, pl.ds(0, 128 * count)],
            (((1,), (1,)), ((), ())),
            preferred_element_type=F32,
        )
        total = total[0 : 3 * nb] + total[3 * nb : 6 * nb]
        sums.append([total[k * nb : (k + 1) * nb] for k in range(3)])
    items = [sums[stream][k] for k in range(3) for stream in range(4)]
    items += [cpack_ref[pl.ds(k * nb, nb), :] for k in range(3)]
    per_row = 128 // cap
    height = buf_ref.shape[0] // nb
    position = lax.broadcasted_iota(jnp.int32, (nb, 128), 1) // cap
    for r in range(height):
        inside = items[r * per_row : (r + 1) * per_row]
        value = inside[0]
        for i, item in enumerate(inside[1:], 1):
            value = jnp.where(position == i, item, value)
        buf_ref[pl.ds(r, nb, stride=height), :] = value
    wait_side(side, grad_ref, gout, sem)


def slot_kernel(nb, cap, blk_ref, coords_ref, mine_ref, cpack_ref, lhs, rhs):
    mine_ref[0:8, :] = blk_ref[...]
    slot_of = (lax.broadcasted_iota(jnp.int32, (128, 128), 0) & (cap - 1)).astype(F32)

    def emit(y, here, rank):
        mine_ref[8 + y : 9 + y, :] = rank
        lanes = pl.ds(128 * y, 128)
        rhs[:, lanes] = jnp.where(jnp.broadcast_to(rank, (128, 128)) == slot_of, 1.0, 0.0).astype(jnp.bfloat16)
        for k in range(3):
            rest = coords_ref[k, y : y + 1, :]
            for part in range(3):
                piece = rest.astype(jnp.bfloat16).astype(F32)
                rest = rest - piece
                lhs[pl.ds((3 * part + k) * nb, nb), lanes] = (
                    here * jnp.broadcast_to(piece, (nb, 128))
                ).astype(jnp.bfloat16)

    block_ranks(nb, [[blk_ref[y : y + 1, :] for y in range(8)]], emit)
    total = lax.dot_general(lhs[...], rhs[...], (((1,), (1,)), ((), ())), preferred_element_type=F32)
    cpack_ref[...] = total[0 : 3 * nb] + total[3 * nb : 6 * nb] + total[6 * nb : 9 * nb]


def powers(t, degree):
    out = [None, t]
    for n in range(2, degree + 1):
        out.append(out[n // 2] * out[n - n // 2])
    return out


def bernstein(t, degree):
    up = powers(t, degree)
    down = powers(1.0 - t, degree)
    out = []
    for a in range(degree + 1):
        if a == 0:
            out.append(down[degree])
        elif a == degree:
            out.append(up[degree])
        else:
            out.append(float(math.comb(degree, a)) * up[a] * down[degree - a])
    return out


def lattice_kernel(nb, cap, py, buf_ref, part_ref, yrow_ref, xrow_ref, owned_ref, out_ref, lhs, rhs):
    rows = lax.broadcasted_iota(jnp.int32, TILE, 0)
    for k in range(3):
        beside = jnp.broadcast_to(yrow_ref[k : k + 1, :], TILE)
        owned_ref[k] = part_ref[0, k] + jnp.where(rows == 0, beside, 0.0) + xrow_ref[k]
    per_row = 128 // cap
    height = buf_ref.shape[0] // nb
    source = lax.broadcasted_iota(jnp.int32, (nb, 128), 0)
    lane = lax.broadcasted_iota(jnp.int32, (16, 128), 1)

    def item(j):
        value = buf_ref[pl.ds(j // per_row, nb, stride=height), :]
        at = j % per_row
        return pltpu.roll(value, 128 - at * cap, 1) if at else value

    def from_px(value):
        return jnp.where(source >= py, pltpu.roll(value, py, 0), 0.0)

    def from_py(value):
        return jnp.where(source % py > 0, pltpu.roll(value, 1, 0), pltpu.roll(value, nb - (py - 1), 0))

    def dense(value):
        out = value[0:16]
        for i in range(1, per_row):
            piece = pltpu.roll(value[16 * i : 16 * (i + 1)], i * cap, 1)
            out = jnp.where(lane // cap == i, piece, out)
        return out

    sens = []
    for k in range(3):
        own, above, beside, across = [item(4 * k + stream) for stream in range(4)]
        sens.append(dense(own + from_py(beside) + from_px(above + from_py(across))))
    u, v, w = [dense(item(12 + k)) for k in range(3)]
    bu = bernstein(u, LU - 1)
    bv = bernstein(v, LV - 1)
    bw = bernstein(w, LW - 1)
    for a in range(LU):
        for k in range(3):
            lhs[pl.ds(16 * (3 * a + k), 16), :] = sens[k] * bu[a]
    for b in range(LV):
        for c in range(LW):
            rhs[pl.ds(16 * (LW * b + c), 16), :] = bv[b] * bw[c]
    left = jnp.concatenate([lhs[pl.ds(i, 3 * LU, stride=16), :] for i in range(16)], axis=1)
    right = jnp.concatenate([rhs[pl.ds(i, LV * LW, stride=16), :] for i in range(16)], axis=1)
    left_high = left.astype(jnp.bfloat16)
    left_low = (left - left_high.astype(F32)).astype(jnp.bfloat16)
    right_high = right.astype(jnp.bfloat16)
    right_low = (right - right_high.astype(F32)).astype(jnp.bfloat16)

    def product(x, y):
        return lax.dot_general(x, y, (((1,), (1,)), ((), ())), preferred_element_type=F32)

    total = product(left_high, right_high) + (product(left_high, right_low) + product(left_low, right_high))
    for a in range(LU):
        for k in range(3):
            out_ref[k, :, pl.ds(LV * LW * a, LV * LW)] = total[3 * a + k : 3 * a + k + 1, :]


TILE = (8, 128)
VMEM = pl.BlockSpec(memory_space=pltpu.VMEM)
HBM = pl.BlockSpec(memory_space=pltpu.HBM)


def near(*arrays):
    return [pltpu.with_memory_space_constraint(array, pltpu.VMEM) for array in arrays]


def volume_call(u, lam, disp, even, odd):
    return pl.pallas_call(
        volume_kernel,
        in_specs=[HBM, HBM, VMEM, VMEM, VMEM],
        out_specs=[HBM, VMEM, VMEM, VMEM, VMEM],
        out_shape=[
            jax.ShapeDtypeStruct((5, 64) + TILE, F32),
            pltpu.VMEM((2, 5, 16) + TILE, F32),
            pltpu.VMEM((2, 5, 16) + TILE, F32),
            pltpu.VMEM((2, 2, 4, 3) + TILE, F32),
            pltpu.VMEM((2, 3, 2) + TILE, F32),
        ],
        scratch_shapes=[
            pltpu.VMEM((5, 64) + TILE, F32),
            pltpu.VMEM((2, 5, 16) + TILE, F32),
            pltpu.VMEM((2, 5, 16) + TILE, F32),
        ]
        + [pltpu.VMEM((4, 4, 3) + TILE, F32)] * 6
        + [
            pltpu.VMEM((4, 16, 5) + TILE, F32),
            pltpu.VMEM((16, 5) + TILE, F32),
            pltpu.VMEM((2, 4, 5) + TILE, F32),
            pltpu.SemaphoreType.DMA((11,)),
        ],
        name="volume",
    )(u, lam, *near(disp, even, odd))


def trace_call(lam, cube, blk, coords, disp):
    return pl.pallas_call(
        trace_kernel,
        in_specs=[HBM] * 5,
        out_specs=[VMEM] * 7,
        out_shape=[
            pltpu.VMEM((5, 16) + TILE, F32),
            pltpu.VMEM((5, 16) + TILE, F32),
            pltpu.VMEM((81, 128), F32),
            pltpu.VMEM((81, 128), F32),
            pltpu.VMEM(TILE, F32),
            pltpu.VMEM((3,) + TILE, F32),
            pltpu.VMEM((27, 2, 128), F32),
        ],
        scratch_shapes=[
            pltpu.VMEM((2, 5, 4, 4) + TILE, F32),
            pltpu.VMEM(TILE, jnp.int32),
            pltpu.SemaphoreType.DMA((7,)),
        ],
        name="traces",
    )(lam, cube, blk, coords, disp)


def first_face_call(grad, u, own, received, gkeep, cols, g):
    return pl.pallas_call(
        first_face_kernel,
        in_specs=[HBM] + [VMEM] * 6,
        out_specs=[HBM, VMEM, VMEM],
        out_shape=[
            jax.ShapeDtypeStruct((5, 64) + TILE, F32),
            pltpu.VMEM((2, 3) + TILE, F32),
            pltpu.VMEM((6, 128), F32),
        ],
        scratch_shapes=[pltpu.VMEM((5, 16) + TILE, F32), pltpu.SemaphoreType.DMA((4,))],
        input_output_aliases={0: 0},
        name="faces_first",
    )(grad, *near(u, own, received, gkeep, cols, g))


def label_call(even, odd, far, rows, nb):
    return pl.pallas_call(
        functools.partial(label_kernel, nb),
        in_specs=[VMEM] * 4,
        out_specs=VMEM,
        out_shape=pltpu.VMEM((32, 128), F32),
        name="labels",
    )(*near(even, odd, far, rows))


def second_face_call(grad, u, own, received, gkeep, cols, g, part, rows, mine, labels, cpack, nb, cap, px):
    height = -(-15 * cap // 128)
    return pl.pallas_call(
        functools.partial(second_face_kernel, nb, cap, px),
        in_specs=[HBM] + [VMEM] * 11,
        out_specs=[HBM, VMEM, VMEM, VMEM],
        out_shape=[
            jax.ShapeDtypeStruct((5, 64) + TILE, F32),
            pltpu.VMEM((nb * height, 128), F32),
            pltpu.VMEM((2, 3) + TILE, F32),
            pltpu.VMEM((6, 128), F32),
        ],
        scratch_shapes=[
            pltpu.VMEM((5, 16) + TILE, F32),
            pltpu.VMEM((6 * nb, 1024), jnp.bfloat16),
            pltpu.VMEM((128, 1024), jnp.bfloat16),
            pltpu.SemaphoreType.DMA((4,)),
        ],
        input_output_aliases={0: 0},
        name="faces_second",
    )(grad, *near(u, own, received, gkeep, cols, g, part, rows, mine, labels, cpack))


def slot_call(blk, coords, nb, cap):
    return pl.pallas_call(
        functools.partial(slot_kernel, nb, cap),
        in_specs=[VMEM, VMEM],
        out_specs=[VMEM, VMEM],
        out_shape=[
            pltpu.VMEM((16, 128), F32),
            pltpu.VMEM((3 * nb, 128), F32),
        ],
        scratch_shapes=[
            pltpu.VMEM((9 * nb, 1024), jnp.bfloat16),
            pltpu.VMEM((128, 1024), jnp.bfloat16),
        ],
        name="slots",
    )(*near(blk, coords))


def lattice_call(buf, part, yrow, xrow, nb, cap, py):
    return pl.pallas_call(
        functools.partial(lattice_kernel, nb, cap, py),
        in_specs=[VMEM] * 4,
        out_shape=[
            jax.ShapeDtypeStruct((3,) + TILE, F32),
            jax.ShapeDtypeStruct((3, 1, LU * LV * LW), F32),
        ],
        scratch_shapes=[
            pltpu.VMEM((16 * 3 * LU, 128), F32),
            pltpu.VMEM((16 * LV * LW, 128), F32),
        ],
        name="lattice",
    )(*near(buf, part, yrow, xrow))


def shift_px(payload, step):
    length = lax.axis_size("px")
    pairs = [(i, i + step) for i in range(length) if 0 <= i + step < length]
    return lax.ppermute(payload, "px", pairs)


def shift_py(payload, step):
    length = lax.axis_size("py")
    return lax.ppermute(payload, "py", [(i, (i + step) % length) for i in range(length)])


def swap(payload, axis, start, wrap):
    length = lax.axis_size(axis)
    pairs = []
    for i in range(start, length, 2):
        j = (i + 1) % length
        if i + 1 < length or wrap:
            pairs += [(i, j), (j, i)]
    return lax.ppermute(payload, axis, pairs)


def per_device(flow_state, adjoint, displacement, lattice_block, lattice_coords):
    px = lax.axis_size("px")
    py = lax.axis_size("py")
    assert px % 2 == 0 and py % 2 == 0
    nb = px * py
    cap = 2 * 1024 // nb
    u = flow_state.reshape(5, 64, 8, 128)
    lam = adjoint.reshape(5, 64, 8, 128)
    own_even, own_odd, y_even, y_odd, blk, coords, disp = trace_call(
        lam,
        adjoint.reshape(5, 4, 4, 4, 8, 128),
        lattice_block.reshape(8, 128),
        lattice_coords.reshape(3, 8, 128),
        displacement.transpose(0, 2, 1, 3).reshape(27, 2, 128),
    )
    first = swap(own_even, "px", 0, False)
    second = swap(own_odd, "px", 1, False)
    even = swap(y_even, "py", 0, True)
    odd = swap(y_odd, "py", 1, True)
    mine, cpack = slot_call(blk, coords, nb, cap)
    beside = jnp.where(lax.axis_index("py") % 2 == 0, even[80:81], odd[80:81])
    far = shift_px(jnp.concatenate([blk, beside]), -1)
    grad, ukeep, gkeep, cols, g = volume_call(u, lam, disp, even, odd)
    grad, part, rows = first_face_call(grad, ukeep, own_even, first, gkeep, cols, g)
    labels = label_call(even, odd, far, rows, nb)
    grad, buf, part, rows = second_face_call(
        grad, ukeep, own_odd, second, gkeep, cols, g, part, rows, mine, labels, cpack, nb, cap, px
    )
    received = lax.all_to_all(buf, ("px", "py"), split_axis=0, concat_axis=0, tiled=True)
    yrow = shift_py(rows, 1)
    below = jnp.pad(yrow[3:6, None, :], ((0, 0), (0, 7), (0, 0)))
    xrow = shift_px(part[1] + below, 1)
    owned, lattice = lattice_call(received, part, yrow, xrow, nb, cap, py)
    return (
        grad.reshape(5, 64, 1, 8, 128),
        owned.reshape(3, 1, 8, 128),
        lattice.reshape(1, 1, 3, LU * LV * LW),
    )


def solution(mesh):
    in_specs = (
        P(None, None, "px", "py", None),
        P(None, None, "px", "py", None),
        P(None, "px", "py", None),
        P("px", "py", None, None),
        P("px", "py", None, None),
    )
    out_specs = (
        P(None, None, "px", "py", None),
        P(None, "px", "py", None),
        P("px", "py", None, None),
    )
    return jax.shard_map(
        per_device, mesh=mesh, in_specs=in_specs, out_specs=out_specs, check_vma=False
    )
```

```python
import functools
import math

import jax
import jax.numpy as jnp
import numpy as np
from jax import lax
from jax.experimental import pallas as pl
from jax.experimental.pallas import tpu as pltpu
from jax.sharding import PartitionSpec as P

LU = 12
LV = 12
LW = 6
F32 = jnp.float32
POINTS = [-1.0, -1.0 / math.sqrt(5.0), 1.0 / math.sqrt(5.0), 1.0]
WEIGHTS = [1.0 / 6.0, 5.0 / 6.0, 5.0 / 6.0, 1.0 / 6.0]
UPPER = [0.5 * (1.0 + point) for point in POINTS]


def derivative_matrix():
    matrix = np.zeros((4, 4))
    for target in range(4):
        for source in range(4):
            others = [m for m in range(4) if m != source]
            if target == source:
                matrix[target, source] = sum(1.0 / (POINTS[source] - POINTS[m]) for m in others)
            else:
                upper = np.prod([POINTS[target] - POINTS[m] for m in others if m != target])
                lower = np.prod([POINTS[source] - POINTS[m] for m in others])
                matrix[target, source] = upper / lower
    return matrix


DM = derivative_matrix()


def line_slopes(line, scale):
    e0 = line[0] + line[3]
    o0 = line[0] - line[3]
    e1 = line[1] + line[2]
    o1 = line[1] - line[2]
    even = e0 - e1
    out = [None] * 4
    for m in range(2):
        half = 0.5 * scale[m]
        p0 = float(half * (DM[m, 0] - DM[m, 3]))
        p1 = float(half * (DM[m, 1] - DM[m, 2]))
        k = float(half * (DM[m, 0] + DM[m, 3]))
        odd_part = p0 * o0 + p1 * o1
        even_part = k * even
        out[m] = odd_part + even_part
        out[3 - m] = odd_part - even_part
    return out


def spread(low, high):
    step = high - low
    return [low, low + float(UPPER[1]) * step, low + float(UPPER[2]) * step, high]


def gather_back(g):
    middle = float(UPPER[1]) * g[1] + float(UPPER[2]) * g[2]
    return (g[0] + g[1] + g[2] - middle, g[3] + middle)


def cross(x, y):
    return [x[1] * y[2] - x[2] * y[1], x[2] * y[0] - x[0] * y[2], x[0] * y[1] - x[1] * y[0]]


def dot3(x, y):
    return x[0] * y[0] + x[1] * y[1] + x[2] * y[2]


def add(x, y):
    return y if x is None else x + y


def add3(x, y):
    return y if x is None else [x[i] + y[i] for i in range(3)]


def primitives(u):
    inverse = 1.0 / u[0]
    v = [u[1] * inverse, u[2] * inverse, u[3] * inverse]
    mv = u[1] * v[0] + u[2] * v[1] + u[3] * v[2]
    p = 0.4 * u[4] - 0.2 * mv
    return inverse, v, mv * inverse, p, u[4] + p


class Node:
    def __init__(self, u):
        self.inverse, self.v, self.v2, self.p, self.ep = primitives(u)
        self.big = [u[0], u[1], u[2], u[3], self.ep]
        self.w = [None] * 5
        self.pb = None
        self.b = None

    def work(self, s):
        return sum((s[f] * self.big[f] for f in range(1, 5)), s[0] * self.big[0])

    def volume(self, adj, s, vn):
        back = []
        for d in range(3):
            k = self.work(s[d])
            for f in range(5):
                self.w[f] = add(self.w[f], vn[d] * s[d][f])
            self.pb = add(self.pb, dot3(adj[d], s[d][1:4]))
            self.b = add3(self.b, [adj[d][c] * k for c in range(3)])
            back.append([self.v[c] * k + self.p * s[d][1 + c] for c in range(3)])
        self.pb = self.pb + self.w[4]
        return back

    def face(self, n, vn, jump, sigma):
        k = self.work(jump)
        square = dot3(n, n)
        root = lax.rsqrt(square)
        twice = 2.0 * root
        length = twice * square
        if isinstance(sigma, int) and sigma == 1:
            cf = vn + length
        elif isinstance(sigma, int):
            cf = vn - length
            twice = -twice
        else:
            cf = vn + sigma * length
            twice = sigma * twice
        q = k - jump[4] * self.p
        along = twice * q
        for f in range(5):
            self.w[f] = add(self.w[f], cf * jump[f])
        self.pb = add(self.pb, dot3(n, jump[1:4]) + vn * jump[4])
        self.b = add3(self.b, [n[c] * k for c in range(3)])
        return [self.v[c] * k + self.p * jump[1 + c] + n[c] * along for c in range(3)]

    def gradient(self):
        pb4 = 0.4 * self.pb
        rb = [self.b[c] * self.inverse for c in range(3)]
        out = [self.w[0] - dot3(self.v, rb) + (0.5 * pb4) * self.v2]
        for c in range(3):
            out.append(self.w[1 + c] + rb[c] - pb4 * self.v[c])
        out.append(self.w[4] + pb4)
        return out


def corner(disp_ref, c, e1, e2):
    return disp_ref[pl.ds(9 * c + e2, 8), e1, :]


def with_next(window):
    return [window, pltpu.roll(window, 127, 1)]


def trace_kernel(lam_ref, cube_ref, blk_ref, coords_ref, disp_ref, own_even, own_odd, y_even, y_odd, blkf, coords, disp, tiles, blocks, sem):
    x_odd = lax.axis_index("px") % 2
    y_up = 1 - lax.axis_index("py") % 2
    copies = [
        pltpu.make_async_copy(lam_ref.at[:, pl.ds(48 - 48 * x_odd, 16)], own_even, sem.at[0]),
        pltpu.make_async_copy(lam_ref.at[:, pl.ds(48 * x_odd, 16)], own_odd, sem.at[1]),
        pltpu.make_async_copy(cube_ref.at[:, :, 0, :, pl.ds(0, 1)], tiles.at[0, :, :, :, pl.ds(0, 1)], sem.at[2]),
        pltpu.make_async_copy(cube_ref.at[:, :, 3, :, pl.ds(7, 1)], tiles.at[1, :, :, :, pl.ds(7, 1)], sem.at[3]),
        pltpu.make_async_copy(blk_ref, blocks, sem.at[4]),
        pltpu.make_async_copy(coords_ref, coords, sem.at[5]),
        pltpu.make_async_copy(disp_ref, disp, sem.at[6]),
    ]
    for copy in copies:
        copy.start()
    for copy in copies[2:5]:
        copy.wait()
    blkf[...] = blocks[...].astype(F32)
    rows = tiles.reshape(1280, 128)
    bottom = rows[pl.ds(0, 80, stride=8), :]
    top = rows[pl.ds(640 + 7, 80, stride=8), :]
    y_even[0:80, :] = jnp.where(y_up == 1, top, bottom)
    y_odd[0:80, :] = jnp.where(y_up == 1, bottom, top)
    first_row = blocks[0:1, :].astype(F32)
    y_even[80:81, :] = first_row
    y_odd[80:81, :] = first_row
    for copy in copies[:2] + copies[5:]:
        copy.wait()


def own_slots(nb, cap, blk_ref, coords_ref, mine_ref, cpack_ref, lhs, rhs):
    mine_ref[0:8, :] = blk_ref[...]
    slot_of = (lax.broadcasted_iota(jnp.int32, (128, 128), 0) & (cap - 1)).astype(F32)

    def emit(y, here, rank):
        mine_ref[8 + y : 9 + y, :] = rank
        lanes = pl.ds(128 * y, 128)
        rhs[:, lanes] = jnp.where(jnp.broadcast_to(rank, (128, 128)) == slot_of, 1.0, 0.0).astype(jnp.bfloat16)
        for k in range(3):
            rest = coords_ref[k, y : y + 1, :]
            for part in range(3):
                piece = rest.astype(jnp.bfloat16).astype(F32)
                rest = rest - piece
                lhs[pl.ds((3 * part + k) * nb, nb), lanes] = (
                    here * jnp.broadcast_to(piece, (nb, 128))
                ).astype(jnp.bfloat16)

    block_ranks(nb, [[blk_ref[y : y + 1, :] for y in range(8)]], emit)
    total = lax.dot_general(lhs[...], rhs[...], (((1,), (1,)), ((), ())), preferred_element_type=F32)
    cpack_ref[...] = total[0 : 3 * nb] + total[3 * nb : 6 * nb] + total[6 * nb : 9 * nb]


def volume_kernel(nb, cap, u_ref, lam_ref, disp_ref, even_ref, odd_ref, blk_ref, coords_ref, grad_ref, lkeep, ukeep, gkeep, cols, g_ref, mine_ref, cpack_ref, lam, umid, gmid, j0t, j1t, j2t, j0b, j1b, j2b, s1, s2, yj, lhs, rhs, sem):
    lam_copies = [pltpu.make_async_copy(lam_ref.at[f], lam.at[f], sem.at[f]) for f in range(5)]
    u_at = [ukeep.at[0], umid.at[0], umid.at[1], ukeep.at[1]]
    g_at = [gkeep.at[0], gmid.at[0], gmid.at[1], gkeep.at[1]]
    u_copies = [pltpu.make_async_copy(u_ref.at[:, pl.ds(16 * a, 16)], u_at[a], sem.at[5 + a]) for a in range(4)]
    keep_copies = [
        pltpu.make_async_copy(lam_ref.at[:, pl.ds(48 * side, 16)], lkeep.at[side], sem.at[11 + side])
        for side in range(2)
    ]
    for copy in lam_copies + u_copies + keep_copies:
        copy.start()
    own_slots(nb, cap, blk_ref, coords_ref, mine_ref, cpack_ref, lhs, rhs)

    for c in range(3):
        x = [[with_next(corner(disp_ref, c, e1, e2)) for e2 in range(2)] for e1 in range(2)]
        for d in range(3):
            ends = []
            for i in range(2):
                pair = []
                for j in range(2):
                    low = [(0, i, j), (i, 0, j), (i, j, 0)][d]
                    high = [(1, i, j), (i, 1, j), (i, j, 1)][d]
                    half = 0.5 * (x[high[0]][high[1]][high[2]] - x[low[0]][low[1]][low[2]])
                    pair.append(half + 0.5 if c == d else half)
                ends.append(spread(pair[0], pair[1]))
            for j in range(4):
                values = spread(ends[0][j], ends[1][j])
                for i in range(4):
                    [j0t, j1t, j2t][d][i, j, c] = values[i]
                    if d and i in (0, 3):
                        cols[i // 3, d - 1, j, c] = values[i]
    for f in range(5):
        lam_copies[f].wait()
        for b in range(4):
            for c in range(4):
                line = [lam[f, 16 * i + 4 * b + c] for i in range(4)]
                out = line_slopes(line, [-WEIGHTS[i] * WEIGHTS[b] * WEIGHTS[c] for i in range(4)])
                for i in range(4):
                    s1[i, 4 * b + c, f] = out[i]

    above_even = lax.axis_index("py") % 2 == 0
    rows = lax.broadcasted_iota(jnp.int32, (8, 128), 0)
    first_row = rows == 0
    last_row = rows == 7
    mid_copies = []
    for a in range(4):
        base = 16 * a
        wa = WEIGHTS[a]
        u_copies[a].wait()
        for f in range(5):
            for c in range(4):
                line = [lam[f, base + 4 * b + c] for b in range(4)]
                out = line_slopes(line, [-wa * WEIGHTS[b] * WEIGHTS[c] for b in range(4)])
                for b in range(4):
                    s2[4 * b + c, f] = out[b]
                half = float(0.5 * wa * WEIGHTS[c])
                at = f * 16 + a * 4 + c
                one = jnp.broadcast_to(even_ref[at : at + 1, :], TILE)
                two = jnp.broadcast_to(odd_ref[at : at + 1, :], TILE)
                above = jnp.where(above_even, one, two)
                below = jnp.where(above_even, two, one)
                plus = jnp.where(last_row, above, pltpu.roll(line[0], 7, 0))
                top = half * (line[3] - plus)
                bottom = half * (below - line[0])
                yj[1, c, f] = top
                yj[0, c, f] = jnp.where(first_row, bottom, pltpu.roll(top, 1, 0))
        for b in range(4):
            slopes3 = []
            ztop = []
            zbot = []
            half = float(0.5 * wa * WEIGHTS[b])
            for f in range(5):
                line = [lam[f, base + 4 * b + c] for c in range(4)]
                slopes3.append(line_slopes(line, [-wa * WEIGHTS[b] * WEIGHTS[c] for c in range(4)]))
                top = half * (line[3] - pltpu.roll(line[0], 127, 1))
                ztop.append(top)
                zbot.append(pltpu.roll(top, 1, 1))
            back2 = None
            col2 = [j2t[a, b, k] for k in range(3)]
            for c in range(4):
                n = 4 * b + c
                node = Node([u_at[a][f, n] for f in range(5)])
                col0 = [j0t[b, c, k] for k in range(3)]
                col1 = [j1t[a, c, k] for k in range(3)]
                adj = [cross(col1, col2), cross(col2, col0), cross(col0, col1)]
                s = [[s1[a, n, f] for f in range(5)], [s2[n, f] for f in range(5)], [slopes3[f][c] for f in range(5)]]
                vn = [dot3(adj[d], node.v) for d in range(3)]
                back = node.volume(adj, s, vn)
                if b == 0:
                    back[1] = add3(back[1], node.face(adj[1], vn[1], [yj[0, c, f] for f in range(5)], -1))
                if b == 3:
                    back[1] = add3(back[1], node.face(adj[1], vn[1], [yj[1, c, f] for f in range(5)], 1))
                if c == 0:
                    back[2] = add3(back[2], node.face(adj[2], vn[2], zbot, -1))
                if c == 3:
                    back[2] = add3(back[2], node.face(adj[2], vn[2], ztop, 1))
                grads = node.gradient()
                for f in range(5):
                    g_at[a][f, n] = grads[f]
                back0 = add3(cross(back[1], col2), cross(col1, back[2]))
                back1 = add3(cross(col2, back[0]), cross(back[2], col0))
                back2 = add3(back2, add3(cross(back[0], col1), cross(col0, back[1])))
                for k in range(3):
                    j0b[b, c, k] = back0[k] if a == 0 else j0b[b, c, k] + back0[k]
                    j1b[a, c, k] = back1[k] if b == 0 else j1b[a, c, k] + back1[k]
            for k in range(3):
                j2b[a, b, k] = back2[k]
        if a in (1, 2):
            copy = pltpu.make_async_copy(gmid.at[a - 1], grad_ref.at[:, pl.ds(base, 16)], sem.at[8 + a])
            copy.start()
            mid_copies.append(copy)

    for c in range(3):
        gx = [[[None, None], [None, None]], [[None, None], [None, None]]]
        for d in range(3):
            table = [j0b, j1b, j2b][d]
            ends = [[], []]
            for i in range(4):
                low, high = gather_back([table[i, j, c] for j in range(4)])
                ends[0].append(low)
                ends[1].append(high)
            for j in range(2):
                pair = gather_back(ends[j])
                for i in range(2):
                    half = 0.5 * pair[i]
                    low = [(0, i, j), (i, 0, j), (i, j, 0)][d]
                    high = [(1, i, j), (i, 1, j), (i, j, 1)][d]
                    gx[high[0]][high[1]][high[2]] = add(gx[high[0]][high[1]][high[2]], half)
                    gx[low[0]][low[1]][low[2]] = add(gx[low[0]][low[1]][low[2]], -half)
        for e1 in range(2):
            for e2 in range(2):
                g_ref[e1, c, e2] = gx[e1][e2][0] + pltpu.roll(gx[e1][e2][1], 1, 1)
    for copy in mid_copies + keep_copies:
        copy.wait()


def one_side(side, scale, sigma, wall, u_ref, own_ref, received_ref, gkeep, cols, g_ref, grad_ref, part_ref, row_ref, gout, sem):
    col1 = [[cols[side, 0, c, k] for k in range(3)] for c in range(4)]
    back1 = [None] * 4
    back2 = [None] * 4
    for b in range(4):
        col2 = [cols[side, 1, b, k] for k in range(3)]
        for c in range(4):
            n = 4 * b + c
            weight = float(WEIGHTS[b] * WEIGHTS[c])
            u = [u_ref[side, f, n] for f in range(5)]
            own = [own_ref[side, f, n] for f in range(5)]
            normal = cross(col1[c], col2)
            if wall:
                inverse, v, v2, p, ep = primitives(u)
                vn = dot3(normal, v)
                m = u[1:4]
                jump = [-weight * own[f] for f in range(1, 4)]
                square = dot3(normal, normal)
                root = lax.rsqrt(square)
                rate = vn * (root * root)
                q = u[0] * vn
                level = dot3(jump, normal)
                slope = 2.0 * (rate - root)
                phi = q * (rate - 2.0 * root) + p
                lk = level * slope
                along = lk * q * (root * root)
                grads = [level * (0.2 * v2 - rate * vn)]
                for k in range(3):
                    grads.append(lk * normal[k] - (0.4 * level) * v[k])
                grads.append(0.4 * level)
                back = [jump[k] * phi + lk * m[k] - along * normal[k] for k in range(3)]
            else:
                node = Node(u)
                vn = dot3(normal, node.v)
                factor = scale * weight
                jump = [factor * (own[f] - received_ref[f, n]) for f in range(5)]
                back = node.face(normal, vn, jump, sigma)
                grads = node.gradient()
            for f in range(5):
                gout[side, f, n] = gkeep[side, f, n] + grads[f]
            back1[c] = add3(back1[c], cross(col2, back))
            back2[b] = add3(back2[b], cross(back, col1[c]))
        pltpu.make_async_copy(
            gout.at[side, :, pl.ds(4 * b, 4)], grad_ref.at[:, pl.ds(48 * side + 4 * b, 4)], sem.at[side, b]
        ).start()
    rows = lax.broadcasted_iota(jnp.int32, TILE, 0)
    for k in range(3):
        low1, high1 = gather_back([back1[i][k] for i in range(4)])
        low2, high2 = gather_back([back2[i][k] for i in range(4)])
        gx = [[-0.5 * (low1 + low2), 0.5 * (low2 - high1)], [0.5 * (low1 - high2), 0.5 * (high1 + high2)]]
        near = g_ref[side, k, 0] + gx[0][0] + pltpu.roll(gx[0][1], 1, 1)
        far = g_ref[side, k, 1] + gx[1][0] + pltpu.roll(gx[1][1], 1, 1)
        part_ref[side, k] = near + jnp.where(rows == 0, 0.0, pltpu.roll(far, 1, 0))
        row_ref[pl.ds(3 * side + k, 1), :] = far[7:8, :]


def wait_side(side, grad_ref, gout, sem):
    for b in range(4):
        pltpu.make_async_copy(
            gout.at[side, :, pl.ds(4 * b, 4)], grad_ref.at[:, pl.ds(48 * side + 4 * b, 4)], sem.at[side, b]
        ).wait()


def block_ranks(nb, groups, emit):
    block_of = lax.broadcasted_iota(jnp.int32, (nb, 128), 0).astype(F32)
    k_of = lax.broadcasted_iota(jnp.int32, (128, 256), 0)
    z_of = lax.broadcasted_iota(jnp.int32, (128, 256), 1)
    before = jnp.where((k_of < z_of) | (z_of >= 128), 1.0, 0.0).astype(jnp.bfloat16)
    here = [jnp.where(jnp.broadcast_to(row, (nb, 128)) == block_of, 1.0, 0.0) for row in sum(groups, [])]
    counts = jnp.dot(
        jnp.concatenate(here, axis=0).astype(jnp.bfloat16), before, preferred_element_type=F32
    )
    i = 0
    for group in groups:
        offset = None
        for _ in group:
            mine = counts[nb * i : nb * (i + 1)]
            earlier = mine[:, 0:128] if offset is None else mine[:, 0:128] + offset
            emit(i, here[i], jnp.sum(here[i] * earlier, axis=0, keepdims=True))
            offset = add(offset, mine[:, 128:256])
            i += 1


def far_labels(nb, even_ref, odd_ref, far_ref, label_ref):
    beside = jnp.where(lax.axis_index("py") % 2 == 0, even_ref[80:81, :], odd_ref[80:81, :])
    across = far_ref[8:9, :]
    label_ref[0:8, :] = far_ref[0:8, :]
    label_ref[8:9, :] = beside
    label_ref[9:10, :] = across

    def emit(i, here, rank):
        label_ref[16 + i : 17 + i, :] = rank

    block_ranks(nb, [[far_ref[y : y + 1, :] for y in range(8)], [beside], [across]], emit)


def face_kernel(nb, cap, px, even_recv, odd_recv, grad_in_ref, own_ref, u_ref, gkeep, cols, g_ref, mine_ref, even_ref, odd_ref, far_ref, cpack_ref, grad_ref, buf_ref, part_ref, row_ref, gout, label_ref, lhs, rhs, sem):
    index = lax.axis_index("px")
    side = index % 2
    is_first = index == 0
    is_last = index == px - 1

    def run(at, scale, sigma, wall, received_ref):
        one_side(at, scale, sigma, wall, u_ref, own_ref, received_ref, gkeep, cols, g_ref, grad_ref, part_ref, row_ref, gout, sem)

    sign = jnp.where(side == 1, F32(-1.0), F32(1.0))
    run(1 - side, 0.5 * sign, sign, False, even_recv)

    @pl.when(is_first)
    def _():
        run(side, None, None, True, None)

    @pl.when(jnp.logical_not(is_first))
    def _():
        scale = jnp.where(side == 0, F32(-0.5), jnp.where(is_last, F32(1.0), F32(0.5)))
        sigma = jnp.where(side == 0, F32(-1.0), jnp.where(is_last, F32(0.0), F32(1.0)))
        run(side, scale, sigma, False, odd_recv)

    far_labels(nb, even_ref, odd_ref, far_ref, label_ref)

    block_of = lax.broadcasted_iota(jnp.int32, (nb, 128), 0).astype(F32)
    slot_of = (lax.broadcasted_iota(jnp.int32, (128, 128), 0) & (cap - 1)).astype(F32)
    sums = []
    for stream, count in enumerate((8, 8, 1, 1)):
        for y in range(count):
            block, values, rank = [
                (mine_ref[y : y + 1, :], lambda k: part_ref[0, k, y : y + 1, :], mine_ref[8 + y : 9 + y, :]),
                (label_ref[y : y + 1, :], lambda k: part_ref[1, k, y : y + 1, :], label_ref[16 + y : 17 + y, :]),
                (label_ref[8:9, :], lambda k: row_ref[k : k + 1, :], label_ref[24:25, :]),
                (label_ref[9:10, :], lambda k: row_ref[3 + k : 4 + k, :], label_ref[25:26, :]),
            ][stream]
            lanes = pl.ds(128 * y, 128)
            here = jnp.broadcast_to(block, (nb, 128)) == block_of
            rhs[:, lanes] = jnp.where(jnp.broadcast_to(rank, (128, 128)) == slot_of, 1.0, 0.0).astype(jnp.bfloat16)
            for k in range(3):
                row = values(k)
                high = row.astype(jnp.bfloat16).astype(F32)
                for part, piece in enumerate((high, row - high)):
                    lhs[pl.ds((3 * part + k) * nb, nb), lanes] = jnp.where(
                        here, jnp.broadcast_to(piece, (nb, 128)), 0.0
                    ).astype(jnp.bfloat16)
        total = lax.dot_general(
            lhs[:, pl.ds(0, 128 * count)],
            rhs[:, pl.ds(0, 128 * count)],
            (((1,), (1,)), ((), ())),
            preferred_element_type=F32,
        )
        total = total[0 : 3 * nb] + total[3 * nb : 6 * nb]
        sums.append([total[k * nb : (k + 1) * nb] for k in range(3)])
    items = [sums[stream][k] for k in range(3) for stream in range(4)]
    items += [cpack_ref[pl.ds(k * nb, nb), :] for k in range(3)]
    per_row = 128 // cap
    height = buf_ref.shape[0] // nb
    position = lax.broadcasted_iota(jnp.int32, (nb, 128), 1) // cap
    for r in range(height):
        inside = items[r * per_row : (r + 1) * per_row]
        value = inside[0]
        for i, item in enumerate(inside[1:], 1):
            value = jnp.where(position == i, item, value)
        buf_ref[pl.ds(r, nb, stride=height), :] = value
    for at in range(2):
        wait_side(at, grad_ref, gout, sem)


def powers(t, degree):
    out = [None, t]
    for n in range(2, degree + 1):
        out.append(out[n // 2] * out[n - n // 2])
    return out


def bernstein(t, degree):
    up = powers(t, degree)
    down = powers(1.0 - t, degree)
    out = []
    for a in range(degree + 1):
        if a == 0:
            out.append(down[degree])
        elif a == degree:
            out.append(up[degree])
        else:
            out.append(float(math.comb(degree, a)) * up[a] * down[degree - a])
    return out


def lattice_kernel(nb, cap, py, buf_ref, part_ref, yrow_ref, xrow_ref, owned_ref, out_ref, lhs, rhs):
    rows = lax.broadcasted_iota(jnp.int32, TILE, 0)
    for k in range(3):
        beside = jnp.broadcast_to(yrow_ref[k : k + 1, :], TILE)
        owned_ref[k] = part_ref[0, k] + jnp.where(rows == 0, beside, 0.0) + xrow_ref[k]
    per_row = 128 // cap
    height = buf_ref.shape[0] // nb
    source = lax.broadcasted_iota(jnp.int32, (nb, 128), 0)
    lane = lax.broadcasted_iota(jnp.int32, (16, 128), 1)

    def item(j):
        value = buf_ref[pl.ds(j // per_row, nb, stride=height), :]
        at = j % per_row
        return pltpu.roll(value, 128 - at * cap, 1) if at else value

    def from_px(value):
        return jnp.where(source >= py, pltpu.roll(value, py, 0), 0.0)

    def from_py(value):
        return jnp.where(source % py > 0, pltpu.roll(value, 1, 0), pltpu.roll(value, nb - (py - 1), 0))

    def dense(value):
        out = value[0:16]
        for i in range(1, per_row):
            piece = pltpu.roll(value[16 * i : 16 * (i + 1)], i * cap, 1)
            out = jnp.where(lane // cap == i, piece, out)
        return out

    sens = []
    for k in range(3):
        own, above, beside, across = [item(4 * k + stream) for stream in range(4)]
        sens.append(dense(own + from_py(beside) + from_px(above + from_py(across))))
    u, v, w = [dense(item(12 + k)) for k in range(3)]
    bu = bernstein(u, LU - 1)
    bv = bernstein(v, LV - 1)
    bw = bernstein(w, LW - 1)
    for a in range(LU):
        for k in range(3):
            lhs[pl.ds(16 * (3 * a + k), 16), :] = sens[k] * bu[a]
    for b in range(LV):
        for c in range(LW):
            rhs[pl.ds(16 * (LW * b + c), 16), :] = bv[b] * bw[c]
    lhs[pl.ds(16 * 3 * LU, 64), :] = jnp.zeros((64, 128), F32)
    rows = 3 * LU + 4
    left = jnp.concatenate([lhs[pl.ds(i, rows, stride=16), :] for i in range(16)], axis=1)
    right = jnp.concatenate([rhs[pl.ds(i, LV * LW, stride=16), :] for i in range(16)], axis=1)

    def two_pieces(value):
        high = value.astype(jnp.bfloat16).astype(F32)
        return jnp.concatenate([high, value - high], axis=0).astype(jnp.bfloat16)

    both = lax.dot_general(
        two_pieces(left), two_pieces(right), (((1,), (1,)), ((), ())), preferred_element_type=F32
    )
    count = LV * LW
    total = both[0:rows, 0:count] + (both[0:rows, count : 2 * count] + both[rows : 2 * rows, 0:count])
    for a in range(LU):
        for k in range(3):
            out_ref[k, :, pl.ds(LV * LW * a, LV * LW)] = total[3 * a + k : 3 * a + k + 1, :]


TILE = (8, 128)
VMEM = pl.BlockSpec(memory_space=pltpu.VMEM)
HBM = pl.BlockSpec(memory_space=pltpu.HBM)


def near(*arrays):
    return [pltpu.with_memory_space_constraint(array, pltpu.VMEM) for array in arrays]


def distant(*arrays):
    return [pltpu.with_memory_space_constraint(array, pltpu.HBM) for array in arrays]


def volume_call(u, lam, disp, even, odd, blk, coords, nb, cap):
    return pl.pallas_call(
        functools.partial(volume_kernel, nb, cap),
        in_specs=[HBM, HBM] + [VMEM] * 5,
        out_specs=[HBM] + [VMEM] * 7,
        out_shape=[
            jax.ShapeDtypeStruct((5, 64) + TILE, F32),
            pltpu.VMEM((2, 5, 16) + TILE, F32),
            pltpu.VMEM((2, 5, 16) + TILE, F32),
            pltpu.VMEM((2, 5, 16) + TILE, F32),
            pltpu.VMEM((2, 2, 4, 3) + TILE, F32),
            pltpu.VMEM((2, 3, 2) + TILE, F32),
            pltpu.VMEM((16, 128), F32),
            pltpu.VMEM((3 * nb, 128), F32),
        ],
        scratch_shapes=[
            pltpu.VMEM((5, 64) + TILE, F32),
            pltpu.VMEM((2, 5, 16) + TILE, F32),
            pltpu.VMEM((2, 5, 16) + TILE, F32),
        ]
        + [pltpu.VMEM((4, 4, 3) + TILE, F32)] * 6
        + [
            pltpu.VMEM((4, 16, 5) + TILE, F32),
            pltpu.VMEM((16, 5) + TILE, F32),
            pltpu.VMEM((2, 4, 5) + TILE, F32),
            pltpu.VMEM((9 * nb, 1024), jnp.bfloat16),
            pltpu.VMEM((128, 1024), jnp.bfloat16),
            pltpu.SemaphoreType.DMA((13,)),
        ],
        compiler_params=pltpu.CompilerParams(vmem_limit_bytes=20 * 1024 * 1024),
        name="volume",
    )(*distant(u, lam), *near(disp, even, odd, blk, coords))


def trace_call(lam, cube, blk, coords, disp):
    return pl.pallas_call(
        trace_kernel,
        in_specs=[HBM] * 5,
        out_specs=[VMEM] * 7,
        out_shape=[
            pltpu.VMEM((5, 16) + TILE, F32),
            pltpu.VMEM((5, 16) + TILE, F32),
            pltpu.VMEM((81, 128), F32),
            pltpu.VMEM((81, 128), F32),
            pltpu.VMEM(TILE, F32),
            pltpu.VMEM((3,) + TILE, F32),
            pltpu.VMEM((27, 2, 128), F32),
        ],
        scratch_shapes=[
            pltpu.VMEM((2, 5, 4, 4) + TILE, F32),
            pltpu.VMEM(TILE, jnp.int32),
            pltpu.SemaphoreType.DMA((7,)),
        ],
        compiler_params=pltpu.CompilerParams(vmem_limit_bytes=8 * 1024 * 1024),
        name="traces",
    )(*distant(lam, cube, blk, coords, disp))


def face_call(even_recv, odd_recv, grad, *rest, nb, cap, px):
    height = -(-15 * cap // 128)
    return pl.pallas_call(
        functools.partial(face_kernel, nb, cap, px),
        in_specs=[VMEM, VMEM, HBM] + [VMEM] * 10,
        out_specs=[HBM, VMEM, VMEM, VMEM],
        out_shape=[
            jax.ShapeDtypeStruct((5, 64) + TILE, F32),
            jax.ShapeDtypeStruct((nb * height, 128), F32),
            pltpu.VMEM((2, 3) + TILE, F32),
            pltpu.VMEM((6, 128), F32),
        ],
        scratch_shapes=[
            pltpu.VMEM((2, 5, 16) + TILE, F32),
            pltpu.VMEM((32, 128), F32),
            pltpu.VMEM((6 * nb, 1024), jnp.bfloat16),
            pltpu.VMEM((128, 1024), jnp.bfloat16),
            pltpu.SemaphoreType.DMA((2, 4)),
        ],
        input_output_aliases={2: 0},
        compiler_params=pltpu.CompilerParams(vmem_limit_bytes=12 * 1024 * 1024),
        name="faces",
    )(*near(even_recv, odd_recv), *distant(grad), *near(*rest))


def lattice_call(buf, part, yrow, xrow, nb, cap, py):
    return pl.pallas_call(
        functools.partial(lattice_kernel, nb, cap, py),
        in_specs=[VMEM] * 4,
        out_shape=[
            jax.ShapeDtypeStruct((3,) + TILE, F32),
            jax.ShapeDtypeStruct((3, 1, LU * LV * LW), F32),
        ],
        scratch_shapes=[
            pltpu.VMEM((16 * (3 * LU + 4), 128), F32),
            pltpu.VMEM((16 * LV * LW, 128), F32),
        ],
        compiler_params=pltpu.CompilerParams(vmem_limit_bytes=8 * 1024 * 1024),
        name="lattice",
    )(*near(buf, part, yrow, xrow))


def shift_px(payload, step):
    length = lax.axis_size("px")
    pairs = [(i, i + step) for i in range(length) if 0 <= i + step < length]
    return lax.ppermute(payload, "px", pairs)


def shift_py(payload, step):
    length = lax.axis_size("py")
    return lax.ppermute(payload, "py", [(i, (i + step) % length) for i in range(length)])


def swap(payload, axis, start, wrap):
    length = lax.axis_size(axis)
    pairs = []
    for i in range(start, length, 2):
        j = (i + 1) % length
        if i + 1 < length or wrap:
            pairs += [(i, j), (j, i)]
    return lax.ppermute(payload, axis, pairs)


def per_device(flow_state, adjoint, displacement, lattice_block, lattice_coords):
    px = lax.axis_size("px")
    py = lax.axis_size("py")
    assert px % 2 == 0 and py % 2 == 0
    nb = px * py
    cap = 2 * 1024 // nb
    u = flow_state.reshape(5, 64, 8, 128)
    lam = adjoint.reshape(5, 64, 8, 128)
    own_even, own_odd, y_even, y_odd, blk, coords, disp = trace_call(
        lam,
        adjoint.reshape(5, 4, 4, 4, 8, 128),
        lattice_block.reshape(8, 128),
        lattice_coords.reshape(3, 8, 128),
        displacement.transpose(0, 2, 1, 3).reshape(27, 2, 128),
    )
    first = swap(own_even, "px", 0, False)
    second = swap(own_odd, "px", 1, False)
    even = swap(y_even, "py", 0, True)
    odd = swap(y_odd, "py", 1, True)
    beside = jnp.where(lax.axis_index("py") % 2 == 0, even[80:81], odd[80:81])
    far = shift_px(jnp.concatenate([blk, beside]), -1)
    grad, lkeep, ukeep, gkeep, cols, g, mine, cpack = volume_call(u, lam, disp, even, odd, blk, coords, nb, cap)
    grad, buf, part, rows = face_call(
        first, second, grad, lkeep, ukeep, gkeep, cols, g, mine, even, odd, far, cpack, nb=nb, cap=cap, px=px
    )
    received = lax.all_to_all(buf, ("px", "py"), split_axis=0, concat_axis=0, tiled=True)
    yrow = shift_py(rows, 1)
    below = jnp.pad(yrow[3:6, None, :], ((0, 0), (0, 7), (0, 0)))
    xrow = shift_px(part[1] + below, 1)
    owned, lattice = lattice_call(received, part, yrow, xrow, nb, cap, py)
    return (
        grad.reshape(5, 64, 1, 8, 128),
        owned.reshape(3, 1, 8, 128),
        lattice.reshape(1, 1, 3, LU * LV * LW),
    )


def solution(mesh):
    in_specs = (
        P(None, None, "px", "py", None),
        P(None, None, "px", "py", None),
        P(None, "px", "py", None),
        P("px", "py", None, None),
        P("px", "py", None, None),
    )
    out_specs = (
        P(None, None, "px", "py", None),
        P(None, "px", "py", None),
        P("px", "py", None, None),
    )
    return jax.shard_map(
        per_device, mesh=mesh, in_specs=in_specs, out_specs=out_specs, check_vma=False
    )
```

```python
import functools
import math

import jax
import jax.numpy as jnp
import numpy as np
from jax import lax
from jax.experimental import pallas as pl
from jax.experimental.pallas import tpu as pltpu
from jax.sharding import PartitionSpec as P

LU = 12
LV = 12
LW = 6
F32 = jnp.float32
POINTS = [-1.0, -1.0 / math.sqrt(5.0), 1.0 / math.sqrt(5.0), 1.0]
WEIGHTS = [1.0 / 6.0, 5.0 / 6.0, 5.0 / 6.0, 1.0 / 6.0]
UPPER = [0.5 * (1.0 + point) for point in POINTS]


def derivative_matrix():
    matrix = np.zeros((4, 4))
    for target in range(4):
        for source in range(4):
            others = [m for m in range(4) if m != source]
            if target == source:
                matrix[target, source] = sum(1.0 / (POINTS[source] - POINTS[m]) for m in others)
            else:
                upper = np.prod([POINTS[target] - POINTS[m] for m in others if m != target])
                lower = np.prod([POINTS[source] - POINTS[m] for m in others])
                matrix[target, source] = upper / lower
    return matrix


DM = derivative_matrix()


def line_slopes(line, scale):
    e0 = line[0] + line[3]
    o0 = line[0] - line[3]
    e1 = line[1] + line[2]
    o1 = line[1] - line[2]
    even = e0 - e1
    out = [None] * 4
    for m in range(2):
        half = 0.5 * scale[m]
        p0 = float(half * (DM[m, 0] - DM[m, 3]))
        p1 = float(half * (DM[m, 1] - DM[m, 2]))
        k = float(half * (DM[m, 0] + DM[m, 3]))
        odd_part = p0 * o0 + p1 * o1
        even_part = k * even
        out[m] = odd_part + even_part
        out[3 - m] = odd_part - even_part
    return out


def spread(low, high):
    step = high - low
    return [low, low + float(UPPER[1]) * step, low + float(UPPER[2]) * step, high]


def gather_back(g):
    middle = float(UPPER[1]) * g[1] + float(UPPER[2]) * g[2]
    return (g[0] + g[1] + g[2] - middle, g[3] + middle)


def cross(x, y):
    return [x[1] * y[2] - x[2] * y[1], x[2] * y[0] - x[0] * y[2], x[0] * y[1] - x[1] * y[0]]


def dot3(x, y):
    return x[0] * y[0] + x[1] * y[1] + x[2] * y[2]


def add(x, y):
    return y if x is None else x + y


def add3(x, y):
    return y if x is None else [x[i] + y[i] for i in range(3)]


def primitives(u):
    inverse = 1.0 / u[0]
    v = [u[1] * inverse, u[2] * inverse, u[3] * inverse]
    mv = u[1] * v[0] + u[2] * v[1] + u[3] * v[2]
    p = 0.4 * u[4] - 0.2 * mv
    return inverse, v, mv * inverse, p, u[4] + p


class Node:
    def __init__(self, u):
        self.inverse, self.v, self.v2, self.p, self.ep = primitives(u)
        self.big = [u[0], u[1], u[2], u[3], self.ep]
        self.w = [None] * 5
        self.pb = None
        self.b = None

    def work(self, s):
        return sum((s[f] * self.big[f] for f in range(1, 5)), s[0] * self.big[0])

    def volume(self, adj, s, vn):
        back = []
        for d in range(3):
            k = self.work(s[d])
            for f in range(5):
                self.w[f] = add(self.w[f], vn[d] * s[d][f])
            self.pb = add(self.pb, dot3(adj[d], s[d][1:4]))
            self.b = add3(self.b, [adj[d][c] * k for c in range(3)])
            back.append([self.v[c] * k + self.p * s[d][1 + c] for c in range(3)])
        self.pb = self.pb + self.w[4]
        return back

    def face(self, n, vn, jump, sigma):
        k = self.work(jump)
        square = dot3(n, n)
        root = lax.rsqrt(square)
        twice = 2.0 * root
        length = twice * square
        if isinstance(sigma, int) and sigma == 1:
            cf = vn + length
        elif isinstance(sigma, int):
            cf = vn - length
            twice = -twice
        else:
            cf = vn + sigma * length
            twice = sigma * twice
        q = k - jump[4] * self.p
        along = twice * q
        for f in range(5):
            self.w[f] = add(self.w[f], cf * jump[f])
        self.pb = add(self.pb, dot3(n, jump[1:4]) + vn * jump[4])
        self.b = add3(self.b, [n[c] * k for c in range(3)])
        return [self.v[c] * k + self.p * jump[1 + c] + n[c] * along for c in range(3)]

    def gradient(self):
        pb4 = 0.4 * self.pb
        rb = [self.b[c] * self.inverse for c in range(3)]
        out = [self.w[0] - dot3(self.v, rb) + (0.5 * pb4) * self.v2]
        for c in range(3):
            out.append(self.w[1 + c] + rb[c] - pb4 * self.v[c])
        out.append(self.w[4] + pb4)
        return out


def corner(disp_ref, c, e1, e2):
    return disp_ref[pl.ds(9 * c + e2, 8), e1, :]


def with_next(window):
    return [window, pltpu.roll(window, 127, 1)]


def trace_kernel(lam_ref, cube_ref, blk_ref, coords_ref, disp_ref, own_even, own_odd, y_even, y_odd, blkf, coords, disp, tiles, blocks, sem):
    x_odd = lax.axis_index("px") % 2
    y_up = 1 - lax.axis_index("py") % 2
    copies = [
        pltpu.make_async_copy(lam_ref.at[:, pl.ds(48 - 48 * x_odd, 16)], own_even, sem.at[0]),
        pltpu.make_async_copy(lam_ref.at[:, pl.ds(48 * x_odd, 16)], own_odd, sem.at[1]),
        pltpu.make_async_copy(cube_ref.at[:, :, 0, :, pl.ds(0, 1)], tiles.at[0, :, :, :, pl.ds(0, 1)], sem.at[2]),
        pltpu.make_async_copy(cube_ref.at[:, :, 3, :, pl.ds(7, 1)], tiles.at[1, :, :, :, pl.ds(7, 1)], sem.at[3]),
        pltpu.make_async_copy(blk_ref, blocks, sem.at[4]),
        pltpu.make_async_copy(coords_ref, coords, sem.at[5]),
        pltpu.make_async_copy(disp_ref, disp, sem.at[6]),
    ]
    for copy in copies:
        copy.start()
    for copy in copies[2:5]:
        copy.wait()
    blkf[...] = blocks[...].astype(F32)
    rows = tiles.reshape(1920, 128)
    bottom = rows[pl.ds(0, 80, stride=8), :]
    top = rows[pl.ds(640 + 7, 80, stride=8), :]
    y_even[0:80, :] = jnp.where(y_up == 1, top, bottom)
    y_odd[0:80, :] = jnp.where(y_up == 1, bottom, top)
    first_row = blocks[0:1, :].astype(F32)
    y_even[80:81, :] = first_row
    y_odd[80:81, :] = first_row
    for copy in copies[:2] + copies[5:]:
        copy.wait()


def own_slots(nb, cap, blk_ref, coords_ref, mine_ref, cpack_ref, lhs, rhs):
    mine_ref[0:8, :] = blk_ref[...]
    slot_of = (lax.broadcasted_iota(jnp.int32, (128, 128), 0) & (cap - 1)).astype(F32)

    def emit(y, here, rank):
        mine_ref[8 + y : 9 + y, :] = rank
        lanes = pl.ds(128 * y, 128)
        rhs[:, lanes] = jnp.where(jnp.broadcast_to(rank, (128, 128)) == slot_of, 1.0, 0.0).astype(jnp.bfloat16)
        for k in range(3):
            rest = coords_ref[k, y : y + 1, :]
            for part in range(3):
                piece = rest.astype(jnp.bfloat16).astype(F32)
                rest = rest - piece
                lhs[pl.ds((3 * part + k) * nb, nb), lanes] = (
                    here * jnp.broadcast_to(piece, (nb, 128))
                ).astype(jnp.bfloat16)

    block_ranks(nb, [[blk_ref[y : y + 1, :] for y in range(8)]], emit)
    total = lax.dot_general(lhs[...], rhs[...], (((1,), (1,)), ((), ())), preferred_element_type=F32)
    cpack_ref[...] = total[0 : 3 * nb] + total[3 * nb : 6 * nb] + total[6 * nb : 9 * nb]


def volume_kernel(nb, cap, u_ref, lam_ref, disp_ref, even_ref, odd_ref, blk_ref, coords_ref, grad_ref, lkeep, ukeep, gkeep, cols, g_ref, mine_ref, cpack_ref, lam, umid, gmid, j0t, j1t, j2t, j0b, j1b, j2b, s1, s2, yj, lhs, rhs, sem):
    lam_copies = [pltpu.make_async_copy(lam_ref.at[f], lam.at[f], sem.at[f]) for f in range(5)]
    u_at = [ukeep.at[0], umid.at[0], umid.at[1], ukeep.at[1]]
    g_at = [gkeep.at[0], gmid.at[0], gmid.at[1], gkeep.at[1]]
    u_copies = [pltpu.make_async_copy(u_ref.at[:, pl.ds(16 * a, 16)], u_at[a], sem.at[5 + a]) for a in range(4)]
    keep_copies = [
        pltpu.make_async_copy(lam_ref.at[:, pl.ds(48 * side, 16)], lkeep.at[side], sem.at[11 + side])
        for side in range(2)
    ]
    for copy in lam_copies + u_copies + keep_copies:
        copy.start()
    own_slots(nb, cap, blk_ref, coords_ref, mine_ref, cpack_ref, lhs, rhs)

    for c in range(3):
        x = [[with_next(corner(disp_ref, c, e1, e2)) for e2 in range(2)] for e1 in range(2)]
        for d in range(3):
            ends = []
            for i in range(2):
                pair = []
                for j in range(2):
                    low = [(0, i, j), (i, 0, j), (i, j, 0)][d]
                    high = [(1, i, j), (i, 1, j), (i, j, 1)][d]
                    half = 0.5 * (x[high[0]][high[1]][high[2]] - x[low[0]][low[1]][low[2]])
                    pair.append(half + 0.5 if c == d else half)
                ends.append(spread(pair[0], pair[1]))
            for j in range(4):
                values = spread(ends[0][j], ends[1][j])
                for i in range(4):
                    [j0t, j1t, j2t][d][i, j, c] = values[i]
                    if d and i in (0, 3):
                        cols[i // 3, d - 1, j, c] = values[i]
    for f in range(5):
        lam_copies[f].wait()
        for b in range(4):
            for c in range(4):
                line = [lam[f, 16 * i + 4 * b + c] for i in range(4)]
                out = line_slopes(line, [-WEIGHTS[i] * WEIGHTS[b] * WEIGHTS[c] for i in range(4)])
                for i in range(4):
                    s1[i, 4 * b + c, f] = out[i]

    above_even = lax.axis_index("py") % 2 == 0
    rows = lax.broadcasted_iota(jnp.int32, (8, 128), 0)
    first_row = rows == 0
    last_row = rows == 7
    mid_copies = []
    for a in range(4):
        base = 16 * a
        wa = WEIGHTS[a]
        u_copies[a].wait()
        for f in range(5):
            for c in range(4):
                line = [lam[f, base + 4 * b + c] for b in range(4)]
                out = line_slopes(line, [-wa * WEIGHTS[b] * WEIGHTS[c] for b in range(4)])
                for b in range(4):
                    s2[4 * b + c, f] = out[b]
                half = float(0.5 * wa * WEIGHTS[c])
                at = f * 16 + a * 4 + c
                one = jnp.broadcast_to(even_ref[at : at + 1, :], TILE)
                two = jnp.broadcast_to(odd_ref[at : at + 1, :], TILE)
                above = jnp.where(above_even, one, two)
                below = jnp.where(above_even, two, one)
                plus = jnp.where(last_row, above, pltpu.roll(line[0], 7, 0))
                top = half * (line[3] - plus)
                bottom = half * (below - line[0])
                yj[1, c, f] = top
                yj[0, c, f] = jnp.where(first_row, bottom, pltpu.roll(top, 1, 0))
        for b in range(4):
            slopes3 = []
            ztop = []
            zbot = []
            half = float(0.5 * wa * WEIGHTS[b])
            for f in range(5):
                line = [lam[f, base + 4 * b + c] for c in range(4)]
                slopes3.append(line_slopes(line, [-wa * WEIGHTS[b] * WEIGHTS[c] for c in range(4)]))
                top = half * (line[3] - pltpu.roll(line[0], 127, 1))
                ztop.append(top)
                zbot.append(pltpu.roll(top, 1, 1))
            back2 = None
            col2 = [j2t[a, b, k] for k in range(3)]
            for c in range(4):
                n = 4 * b + c
                node = Node([u_at[a][f, n] for f in range(5)])
                col0 = [j0t[b, c, k] for k in range(3)]
                col1 = [j1t[a, c, k] for k in range(3)]
                adj = [cross(col1, col2), cross(col2, col0), cross(col0, col1)]
                s = [[s1[a, n, f] for f in range(5)], [s2[n, f] for f in range(5)], [slopes3[f][c] for f in range(5)]]
                vn = [dot3(adj[d], node.v) for d in range(3)]
                back = node.volume(adj, s, vn)
                if b == 0:
                    back[1] = add3(back[1], node.face(adj[1], vn[1], [yj[0, c, f] for f in range(5)], -1))
                if b == 3:
                    back[1] = add3(back[1], node.face(adj[1], vn[1], [yj[1, c, f] for f in range(5)], 1))
                if c == 0:
                    back[2] = add3(back[2], node.face(adj[2], vn[2], zbot, -1))
                if c == 3:
                    back[2] = add3(back[2], node.face(adj[2], vn[2], ztop, 1))
                grads = node.gradient()
                for f in range(5):
                    g_at[a][f, n] = grads[f]
                back0 = add3(cross(back[1], col2), cross(col1, back[2]))
                back1 = add3(cross(col2, back[0]), cross(back[2], col0))
                back2 = add3(back2, add3(cross(back[0], col1), cross(col0, back[1])))
                for k in range(3):
                    j0b[b, c, k] = back0[k] if a == 0 else j0b[b, c, k] + back0[k]
                    j1b[a, c, k] = back1[k] if b == 0 else j1b[a, c, k] + back1[k]
            for k in range(3):
                j2b[a, b, k] = back2[k]
        if a in (1, 2):
            copy = pltpu.make_async_copy(gmid.at[a - 1], grad_ref.at[:, pl.ds(base, 16)], sem.at[8 + a])
            copy.start()
            mid_copies.append(copy)

    for c in range(3):
        gx = [[[None, None], [None, None]], [[None, None], [None, None]]]
        for d in range(3):
            table = [j0b, j1b, j2b][d]
            ends = [[], []]
            for i in range(4):
                low, high = gather_back([table[i, j, c] for j in range(4)])
                ends[0].append(low)
                ends[1].append(high)
            for j in range(2):
                pair = gather_back(ends[j])
                for i in range(2):
                    half = 0.5 * pair[i]
                    low = [(0, i, j), (i, 0, j), (i, j, 0)][d]
                    high = [(1, i, j), (i, 1, j), (i, j, 1)][d]
                    gx[high[0]][high[1]][high[2]] = add(gx[high[0]][high[1]][high[2]], half)
                    gx[low[0]][low[1]][low[2]] = add(gx[low[0]][low[1]][low[2]], -half)
        for e1 in range(2):
            for e2 in range(2):
                g_ref[e1, c, e2] = gx[e1][e2][0] + pltpu.roll(gx[e1][e2][1], 1, 1)
    for copy in mid_copies + keep_copies:
        copy.wait()


def one_side(side, scale, sigma, wall, u_ref, own_ref, received_ref, gkeep, cols, g_ref, grad_ref, part_ref, row_ref, gout, sem):
    col1 = [[cols[side, 0, c, k] for k in range(3)] for c in range(4)]
    back1 = [None] * 4
    back2 = [None] * 4
    for b in range(4):
        col2 = [cols[side, 1, b, k] for k in range(3)]
        for c in range(4):
            n = 4 * b + c
            weight = float(WEIGHTS[b] * WEIGHTS[c])
            u = [u_ref[side, f, n] for f in range(5)]
            own = [own_ref[side, f, n] for f in range(5)]
            normal = cross(col1[c], col2)
            if wall:
                inverse, v, v2, p, ep = primitives(u)
                vn = dot3(normal, v)
                m = u[1:4]
                jump = [-weight * own[f] for f in range(1, 4)]
                square = dot3(normal, normal)
                root = lax.rsqrt(square)
                rate = vn * (root * root)
                q = u[0] * vn
                level = dot3(jump, normal)
                slope = 2.0 * (rate - root)
                phi = q * (rate - 2.0 * root) + p
                lk = level * slope
                along = lk * q * (root * root)
                grads = [level * (0.2 * v2 - rate * vn)]
                for k in range(3):
                    grads.append(lk * normal[k] - (0.4 * level) * v[k])
                grads.append(0.4 * level)
                back = [jump[k] * phi + lk * m[k] - along * normal[k] for k in range(3)]
            else:
                node = Node(u)
                vn = dot3(normal, node.v)
                factor = scale * weight
                jump = [factor * (own[f] - received_ref[f, n]) for f in range(5)]
                back = node.face(normal, vn, jump, sigma)
                grads = node.gradient()
            for f in range(5):
                gout[side, f, n] = gkeep[side, f, n] + grads[f]
            back1[c] = add3(back1[c], cross(col2, back))
            back2[b] = add3(back2[b], cross(back, col1[c]))
        pltpu.make_async_copy(
            gout.at[side, :, pl.ds(4 * b, 4)], grad_ref.at[:, pl.ds(48 * side + 4 * b, 4)], sem.at[side, b]
        ).start()
    rows = lax.broadcasted_iota(jnp.int32, TILE, 0)
    for k in range(3):
        low1, high1 = gather_back([back1[i][k] for i in range(4)])
        low2, high2 = gather_back([back2[i][k] for i in range(4)])
        gx = [[-0.5 * (low1 + low2), 0.5 * (low2 - high1)], [0.5 * (low1 - high2), 0.5 * (high1 + high2)]]
        near = g_ref[side, k, 0] + gx[0][0] + pltpu.roll(gx[0][1], 1, 1)
        far = g_ref[side, k, 1] + gx[1][0] + pltpu.roll(gx[1][1], 1, 1)
        part_ref[side, k] = near + jnp.where(rows == 0, 0.0, pltpu.roll(far, 1, 0))
        row_ref[pl.ds(3 * side + k, 1), :] = far[7:8, :]


def wait_side(side, grad_ref, gout, sem):
    for b in range(4):
        pltpu.make_async_copy(
            gout.at[side, :, pl.ds(4 * b, 4)], grad_ref.at[:, pl.ds(48 * side + 4 * b, 4)], sem.at[side, b]
        ).wait()


def block_ranks(nb, groups, emit):
    block_of = lax.broadcasted_iota(jnp.int32, (nb, 128), 0).astype(F32)
    k_of = lax.broadcasted_iota(jnp.int32, (128, 256), 0)
    z_of = lax.broadcasted_iota(jnp.int32, (128, 256), 1)
    before = jnp.where((k_of < z_of) | (z_of >= 128), 1.0, 0.0).astype(jnp.bfloat16)
    here = [jnp.where(jnp.broadcast_to(row, (nb, 128)) == block_of, 1.0, 0.0) for row in sum(groups, [])]
    counts = jnp.dot(
        jnp.concatenate(here, axis=0).astype(jnp.bfloat16), before, preferred_element_type=F32
    )
    i = 0
    for group in groups:
        offset = None
        for _ in group:
            mine = counts[nb * i : nb * (i + 1)]
            earlier = mine[:, 0:128] if offset is None else mine[:, 0:128] + offset
            emit(i, here[i], jnp.sum(here[i] * earlier, axis=0, keepdims=True))
            offset = add(offset, mine[:, 128:256])
            i += 1


def far_labels(nb, even_ref, odd_ref, far_ref, label_ref):
    beside = jnp.where(lax.axis_index("py") % 2 == 0, even_ref[80:81, :], odd_ref[80:81, :])
    across = far_ref[8:9, :]
    label_ref[0:8, :] = far_ref[0:8, :]
    label_ref[8:9, :] = beside
    label_ref[9:10, :] = across

    def emit(i, here, rank):
        label_ref[16 + i : 17 + i, :] = rank

    block_ranks(nb, [[far_ref[y : y + 1, :] for y in range(8)], [beside], [across]], emit)


def face_kernel(nb, cap, px, even_recv, odd_recv, grad_in_ref, own_ref, u_ref, gkeep, cols, g_ref, mine_ref, even_ref, odd_ref, far_ref, cpack_ref, grad_ref, buf_ref, part_ref, row_ref, gout, label_ref, lhs, rhs, sem):
    index = lax.axis_index("px")
    side = index % 2
    is_first = index == 0
    is_last = index == px - 1

    def run(at, scale, sigma, wall, received_ref):
        one_side(at, scale, sigma, wall, u_ref, own_ref, received_ref, gkeep, cols, g_ref, grad_ref, part_ref, row_ref, gout, sem)

    sign = jnp.where(side == 1, F32(-1.0), F32(1.0))
    run(1 - side, 0.5 * sign, sign, False, even_recv)

    @pl.when(is_first)
    def _():
        run(side, None, None, True, None)

    @pl.when(jnp.logical_not(is_first))
    def _():
        scale = jnp.where(side == 0, F32(-0.5), jnp.where(is_last, F32(1.0), F32(0.5)))
        sigma = jnp.where(side == 0, F32(-1.0), jnp.where(is_last, F32(0.0), F32(1.0)))
        run(side, scale, sigma, False, odd_recv)

    far_labels(nb, even_ref, odd_ref, far_ref, label_ref)

    block_of = lax.broadcasted_iota(jnp.int32, (nb, 128), 0).astype(F32)
    slot_of = (lax.broadcasted_iota(jnp.int32, (128, 128), 0) & (cap - 1)).astype(F32)
    sums = []
    for stream, count in enumerate((8, 8, 1, 1)):
        for y in range(count):
            block, values, rank = [
                (mine_ref[y : y + 1, :], lambda k: part_ref[0, k, y : y + 1, :], mine_ref[8 + y : 9 + y, :]),
                (label_ref[y : y + 1, :], lambda k: part_ref[1, k, y : y + 1, :], label_ref[16 + y : 17 + y, :]),
                (label_ref[8:9, :], lambda k: row_ref[k : k + 1, :], label_ref[24:25, :]),
                (label_ref[9:10, :], lambda k: row_ref[3 + k : 4 + k, :], label_ref[25:26, :]),
            ][stream]
            lanes = pl.ds(128 * y, 128)
            here = jnp.broadcast_to(block, (nb, 128)) == block_of
            rhs[:, lanes] = jnp.where(jnp.broadcast_to(rank, (128, 128)) == slot_of, 1.0, 0.0).astype(jnp.bfloat16)
            for k in range(3):
                row = values(k)
                high = row.astype(jnp.bfloat16).astype(F32)
                for part, piece in enumerate((high, row - high)):
                    lhs[pl.ds((3 * part + k) * nb, nb), lanes] = jnp.where(
                        here, jnp.broadcast_to(piece, (nb, 128)), 0.0
                    ).astype(jnp.bfloat16)
        total = lax.dot_general(
            lhs[:, pl.ds(0, 128 * count)],
            rhs[:, pl.ds(0, 128 * count)],
            (((1,), (1,)), ((), ())),
            preferred_element_type=F32,
        )
        total = total[0 : 3 * nb] + total[3 * nb : 6 * nb]
        sums.append([total[k * nb : (k + 1) * nb] for k in range(3)])
    items = [sums[stream][k] for k in range(3) for stream in range(4)]
    items += [cpack_ref[pl.ds(k * nb, nb), :] for k in range(3)]
    per_row = 128 // cap
    height = buf_ref.shape[0] // nb
    position = lax.broadcasted_iota(jnp.int32, (nb, 128), 1) // cap
    for r in range(height):
        inside = items[r * per_row : (r + 1) * per_row]
        value = inside[0]
        for i, item in enumerate(inside[1:], 1):
            value = jnp.where(position == i, item, value)
        buf_ref[pl.ds(r, nb, stride=height), :] = value
    for at in range(2):
        wait_side(at, grad_ref, gout, sem)


def powers(t, degree):
    out = [None, t]
    for n in range(2, degree + 1):
        out.append(out[n // 2] * out[n - n // 2])
    return out


def bernstein(t, degree):
    up = powers(t, degree)
    down = powers(1.0 - t, degree)
    out = []
    for a in range(degree + 1):
        if a == 0:
            out.append(down[degree])
        elif a == degree:
            out.append(up[degree])
        else:
            out.append(float(math.comb(degree, a)) * up[a] * down[degree - a])
    return out


def lattice_kernel(nb, cap, py, buf_ref, part_ref, yrow_ref, xrow_ref, owned_ref, out_ref, lhs, rhs):
    rows = lax.broadcasted_iota(jnp.int32, TILE, 0)
    for k in range(3):
        beside = jnp.broadcast_to(yrow_ref[k : k + 1, :], TILE)
        owned_ref[k] = part_ref[0, k] + jnp.where(rows == 0, beside, 0.0) + xrow_ref[pl.ds(8 * k, 8), :]
    per_row = 128 // cap
    height = buf_ref.shape[0] // nb
    source = lax.broadcasted_iota(jnp.int32, (nb, 128), 0)
    lane = lax.broadcasted_iota(jnp.int32, (16, 128), 1)

    def item(j):
        value = buf_ref[pl.ds(j // per_row, nb, stride=height), :]
        at = j % per_row
        return pltpu.roll(value, 128 - at * cap, 1) if at else value

    def from_px(value):
        return jnp.where(source >= py, pltpu.roll(value, py, 0), 0.0)

    def from_py(value):
        return jnp.where(source % py > 0, pltpu.roll(value, 1, 0), pltpu.roll(value, nb - (py - 1), 0))

    def dense(value):
        out = value[0:16]
        for i in range(1, per_row):
            piece = pltpu.roll(value[16 * i : 16 * (i + 1)], i * cap, 1)
            out = jnp.where(lane // cap == i, piece, out)
        return out

    sens = []
    for k in range(3):
        own, above, beside, across = [item(4 * k + stream) for stream in range(4)]
        sens.append(dense(own + from_py(beside) + from_px(above + from_py(across))))
    u, v, w = [dense(item(12 + k)) for k in range(3)]
    bu = bernstein(u, LU - 1)
    bv = bernstein(v, LV - 1)
    bw = bernstein(w, LW - 1)
    for a in range(LU):
        for k in range(3):
            lhs[pl.ds(16 * (3 * a + k), 16), :] = sens[k] * bu[a]
    for b in range(LV):
        for c in range(LW):
            rhs[pl.ds(16 * (LW * b + c), 16), :] = bv[b] * bw[c]
    lhs[pl.ds(16 * 3 * LU, 64), :] = jnp.zeros((64, 128), F32)
    rows = 3 * LU + 4
    left = jnp.concatenate([lhs[pl.ds(i, rows, stride=16), :] for i in range(16)], axis=1)
    right = jnp.concatenate([rhs[pl.ds(i, LV * LW, stride=16), :] for i in range(16)], axis=1)

    def two_pieces(value):
        high = value.astype(jnp.bfloat16).astype(F32)
        return jnp.concatenate([high, value - high], axis=0).astype(jnp.bfloat16)

    both = lax.dot_general(
        two_pieces(left), two_pieces(right), (((1,), (1,)), ((), ())), preferred_element_type=F32
    )
    count = LV * LW
    total = both[0:rows, 0:count] + (both[0:rows, count : 2 * count] + both[rows : 2 * rows, 0:count])
    for a in range(LU):
        for k in range(3):
            out_ref[k, :, pl.ds(LV * LW * a, LV * LW)] = total[3 * a + k : 3 * a + k + 1, :]


TILE = (8, 128)
VMEM = pl.BlockSpec(memory_space=pltpu.VMEM)
HBM = pl.BlockSpec(memory_space=pltpu.HBM)


def near(*arrays):
    return [pltpu.with_memory_space_constraint(array, pltpu.VMEM) for array in arrays]


def distant(*arrays):
    return [pltpu.with_memory_space_constraint(array, pltpu.HBM) for array in arrays]


def volume_call(u, lam, disp, even, odd, blk, coords, nb, cap):
    return pl.pallas_call(
        functools.partial(volume_kernel, nb, cap),
        in_specs=[HBM, HBM] + [VMEM] * 5,
        out_specs=[HBM] + [VMEM] * 7,
        out_shape=[
            jax.ShapeDtypeStruct((5, 64) + TILE, F32),
            pltpu.VMEM((2, 5, 16) + TILE, F32),
            pltpu.VMEM((2, 5, 16) + TILE, F32),
            pltpu.VMEM((2, 5, 16) + TILE, F32),
            pltpu.VMEM((2, 2, 4, 3) + TILE, F32),
            pltpu.VMEM((2, 3, 2) + TILE, F32),
            pltpu.VMEM((16, 128), F32),
            pltpu.VMEM((3 * nb, 128), F32),
        ],
        scratch_shapes=[
            pltpu.VMEM((5, 64) + TILE, F32),
            pltpu.VMEM((2, 5, 16) + TILE, F32),
            pltpu.VMEM((2, 5, 16) + TILE, F32),
        ]
        + [pltpu.VMEM((4, 4, 3) + TILE, F32)] * 6
        + [
            pltpu.VMEM((4, 16, 5) + TILE, F32),
            pltpu.VMEM((16, 5) + TILE, F32),
            pltpu.VMEM((2, 4, 5) + TILE, F32),
            pltpu.VMEM((9 * nb, 1024), jnp.bfloat16),
            pltpu.VMEM((128, 1024), jnp.bfloat16),
            pltpu.SemaphoreType.DMA((13,)),
        ],
        compiler_params=pltpu.CompilerParams(vmem_limit_bytes=20 * 1024 * 1024),
        name="volume",
    )(*distant(u, lam), *near(disp, even, odd, blk, coords))


def trace_call(lam, cube, blk, coords, disp):
    return pl.pallas_call(
        trace_kernel,
        in_specs=[HBM] * 5,
        out_specs=[VMEM] * 7,
        out_shape=[
            pltpu.VMEM((5, 16) + TILE, F32),
            pltpu.VMEM((5, 16) + TILE, F32),
            pltpu.VMEM((81, 128), F32),
            pltpu.VMEM((81, 128), F32),
            pltpu.VMEM(TILE, F32),
            pltpu.VMEM((3,) + TILE, F32),
            pltpu.VMEM((27, 2, 128), F32),
        ],
        scratch_shapes=[
            pltpu.VMEM((3, 5, 4, 4) + TILE, F32),
            pltpu.VMEM(TILE, jnp.int32),
            pltpu.SemaphoreType.DMA((7,)),
        ],
        compiler_params=pltpu.CompilerParams(vmem_limit_bytes=8 * 1024 * 1024),
        name="traces",
    )(*distant(lam, cube, blk, coords, disp))


def face_call(even_recv, odd_recv, grad, *rest, nb, cap, px):
    height = -(-15 * cap // 128)
    return pl.pallas_call(
        functools.partial(face_kernel, nb, cap, px),
        in_specs=[VMEM, VMEM, HBM] + [VMEM] * 10,
        out_specs=[HBM, VMEM, VMEM, VMEM],
        out_shape=[
            jax.ShapeDtypeStruct((5, 64) + TILE, F32),
            jax.ShapeDtypeStruct((nb * height, 128), F32),
            pltpu.VMEM((2, 3) + TILE, F32),
            pltpu.VMEM((6, 128), F32),
        ],
        scratch_shapes=[
            pltpu.VMEM((2, 5, 16) + TILE, F32),
            pltpu.VMEM((32, 128), F32),
            pltpu.VMEM((6 * nb, 1024), jnp.bfloat16),
            pltpu.VMEM((128, 1024), jnp.bfloat16),
            pltpu.SemaphoreType.DMA((2, 4)),
        ],
        input_output_aliases={2: 0},
        compiler_params=pltpu.CompilerParams(vmem_limit_bytes=12 * 1024 * 1024),
        name="faces",
    )(*near(even_recv, odd_recv), *distant(grad), *near(*rest))


def lattice_call(buf, part, yrow, xrow, nb, cap, py):
    return pl.pallas_call(
        functools.partial(lattice_kernel, nb, cap, py),
        in_specs=[VMEM] * 4,
        out_shape=[
            jax.ShapeDtypeStruct((3,) + TILE, F32),
            jax.ShapeDtypeStruct((3, 1, LU * LV * LW), F32),
        ],
        scratch_shapes=[
            pltpu.VMEM((16 * (3 * LU + 5), 128), F32),
            pltpu.VMEM((16 * (LV * LW + 1), 128), F32),
        ],
        compiler_params=pltpu.CompilerParams(vmem_limit_bytes=8 * 1024 * 1024),
        name="lattice",
    )(*near(buf, part, yrow, xrow))


def shift_px(payload, step):
    length = lax.axis_size("px")
    pairs = [(i, i + step) for i in range(length) if 0 <= i + step < length]
    return lax.ppermute(payload, "px", pairs)


def shift_py(payload, step):
    length = lax.axis_size("py")
    return lax.ppermute(payload, "py", [(i, (i + step) % length) for i in range(length)])


def swap(payload, axis, start, wrap):
    length = lax.axis_size(axis)
    pairs = []
    for i in range(start, length, 2):
        j = (i + 1) % length
        if i + 1 < length or wrap:
            pairs += [(i, j), (j, i)]
    return lax.ppermute(payload, axis, pairs)


def per_device(flow_state, adjoint, displacement, lattice_block, lattice_coords):
    px = lax.axis_size("px")
    py = lax.axis_size("py")
    assert px % 2 == 0 and py % 2 == 0
    nb = px * py
    cap = 2 * 1024 // nb
    u = flow_state.reshape(5, 64, 8, 128)
    lam = adjoint.reshape(5, 64, 8, 128)
    own_even, own_odd, y_even, y_odd, blk, coords, disp = trace_call(
        lam,
        adjoint.reshape(5, 4, 4, 4, 8, 128),
        lattice_block.reshape(8, 128),
        lattice_coords.reshape(3, 8, 128),
        displacement.transpose(0, 2, 1, 3).reshape(27, 2, 128),
    )
    first = swap(own_even, "px", 0, False)
    second = swap(own_odd, "px", 1, False)
    even = swap(y_even, "py", 0, True)
    odd = swap(y_odd, "py", 1, True)
    beside = jnp.where(lax.axis_index("py") % 2 == 0, even[80:81], odd[80:81])
    far = shift_px(jnp.concatenate([blk, beside]), -1)
    grad, lkeep, ukeep, gkeep, cols, g, mine, cpack = volume_call(u, lam, disp, even, odd, blk, coords, nb, cap)
    grad, buf, part, rows = face_call(
        first, second, grad, lkeep, ukeep, gkeep, cols, g, mine, even, odd, far, cpack, nb=nb, cap=cap, px=px
    )
    received = lax.all_to_all(buf, ("px", "py"), split_axis=0, concat_axis=0, tiled=True)
    xrow = shift_px(jnp.concatenate([part[1].reshape(24, 128), rows[3:6]]), 1)
    yrow = shift_py(rows[0:3] + xrow[24:27], 1)
    owned, lattice = lattice_call(received, part, yrow, xrow, nb, cap, py)
    return (
        grad.reshape(5, 64, 1, 8, 128),
        owned.reshape(3, 1, 8, 128),
        lattice.reshape(1, 1, 3, LU * LV * LW),
    )


def solution(mesh):
    in_specs = (
        P(None, None, "px", "py", None),
        P(None, None, "px", "py", None),
        P(None, "px", "py", None),
        P("px", "py", None, None),
        P("px", "py", None, None),
    )
    out_specs = (
        P(None, None, "px", "py", None),
        P(None, "px", "py", None),
        P("px", "py", None, None),
    )
    return jax.shard_map(
        per_device, mesh=mesh, in_specs=in_specs, out_specs=out_specs, check_vma=False
    )
```
